32 devices in a mesh: groups: 2 (over x), ctx: 16 (over z, y, core).
Axes of the slice: x: 2, y: 2, z: 4, core: 2. Of those that a mesh axis runs over, the one named last changes fastest.
Arguments:
- queries: bfloat16 [4096, 2048], P(('groups', 'ctx')), parts along dimension 0, may hold values from -6 to 6
- keys: bfloat16 [8192, 256], P(('groups', 'ctx')), parts along dimension 0, may hold values from -6 to 6
- values: bfloat16 [8192, 256], P(('groups', 'ctx')), parts along dimension 0, may hold values from -6 to 6
- kv_lengths: int32 [32], P(('groups', 'ctx')), parts along dimension 0, may hold values from 1 to 256, 2048 in all
- stream: bfloat16 [4096, 2048], P(('groups', 'ctx')), parts along dimension 0, may hold values from -6 to 6
- out_weight: bfloat16 [2048, 2048], P('ctx'), may hold values from -0.125 to 0.125
- routes: int32 [4096, 8], P(('groups', 'ctx')), parts along dimension 0, may hold values from 0 to 15, all different within a row; in each aligned block of 128 rows (0 to 127, 128 to 255, ...) at most 72 rows name the same one
- gate_weights: float32 [4096, 8], P(('groups', 'ctx')), parts along dimension 0, may hold values from 0.2 to 1
- expert_gate: bfloat16 [16, 2048, 768], P('ctx'), may hold values from -0.125 to 0.125
- expert_up: bfloat16 [16, 2048, 768], P('ctx'), may hold values from -0.125 to 0.125
- expert_down: bfloat16 [16, 768, 2048], P('ctx'), may hold values from -0.21875 to 0.21875
Outputs:
- attended: bfloat16 [4096, 2048], P(('groups', 'ctx')), parts along dimension 0
- layer_out: bfloat16 [4096, 2048], P(('groups', 'ctx')), parts along dimension 0
The draws below stay inside these ranges and needn't reach their ends.
There are 2 independent parts, one for each index of `groups`. The reference program is written for one: setup_inputs(seed, part) draws one part's arguments, and reference() takes and returns one part's arrays. A program takes and returns all parts, laid end to end along the dimension named above; an argument that names none is the same for every part. Nothing has to cross between parts.
Inputs may be any that keep to these rules, and one draw needn't show every extreme that they name: `routes`: in the rows of one device (aligned blocks of 128 rows) no expert is named by more than 72 entries.
All inputs are finite; a program needn't handle non-finite values. No bound on the sum of `kv_lengths` on one device may be relied on, other than what follows from the above.
Results may differ from the reference program's by a relative error of at most 0.015.
Values may be sent and summed in bfloat16 or wider, within the bound.
No kernel may reach another device: no remote copies, remote signals or barrier semaphores. Data moves between devices by JAX's collectives and lax.ppermute only.
A program may use at most 128 MiB of HBM per device.

```python
import math
import jax
import jax.numpy as jnp
import numpy as np
from jax import lax

D = 2048
HD = 128
HEADS = 16
KVH = 2
FFE = 768
TOP = 8
STOPS = 8
QD = 128
KC = 256
EXPERTS = 16
CAP = 72
TOKENS = 2048
KEYS = 4096
N_CTX = 16


def base_values(key, array_shape):
    return jax.random.truncated_normal(key, -3.5, 3.5, array_shape, jnp.float32) * 1.4


def draw_queries(key, part):
    drawn = base_values(jax.random.fold_in(key, 1), (N_CTX, QD, KVH, HEADS // KVH, HD))
    return drawn.reshape(N_CTX * QD, HEADS * HD).astype(jnp.bfloat16)


def draw_keys(key, part):
    drawn = base_values(jax.random.fold_in(key, 2), (N_CTX, KC, KVH, HD))
    return drawn.reshape(N_CTX * KC, KVH * HD).astype(jnp.bfloat16)


def levels(key, dims, pieces, smallest, top_value):
    def one(position, parts):
        draws = jax.random.uniform(jax.random.fold_in(jax.random.fold_in(key, 6), position), (parts,), jnp.float32, smallest / len(pieces), top_value / len(pieces))
        return jnp.repeat(jnp.exp(draws), dims[position] // parts).reshape((-1,) + (1,) * (len(dims) - position - 1))

    level = one(*pieces[0])
    for cut in pieces[1:]:
        level = level * one(*cut)
    return level


def length_profile(amount, total, bound, skew):
    loads = [(1 << 20) // math.isqrt(rank ** skew) + 1 for rank in range(2, amount + 1)]
    spare, counts = total - bound - (amount - 1), [1] * (amount - 1)
    while spare > 0:
        candidates = [i for i in range(amount - 1) if counts[i] < bound]
        whole, left = sum([loads[i] for i in candidates]), spare
        for i in candidates:
            more = min(bound - counts[i], max(1, left * loads[i] // whole), spare)
            counts[i] = counts[i] + more
            spare = spare - more
    return np.array([bound] + counts)


def uneven_parts(stream_key, number_of, total, most, slope):
    if number_of == 2:
        one = jax.random.randint(stream_key, (), max(1, total - most), min(most, total - 1) + 1)
        return jnp.stack([one, total - one])
    sizes = jnp.asarray(length_profile(number_of, total, most, slope), jnp.int32)
    twos = (number_of - 1) // 2
    donor, receiver = sizes[1:1 + 2 * twos:2], sizes[2:2 + 2 * twos:2]
    margin = jnp.minimum(donor - 1, most - receiver)
    shifted = jax.random.randint(jax.random.fold_in(stream_key, 1), (twos,), 0, 1 << 20) % (margin + 1)
    sizes = sizes.at[1:1 + 2 * twos:2].set(donor - shifted).at[2:2 + 2 * twos:2].set(receiver + shifted)
    return sizes[jax.random.permutation(jax.random.fold_in(stream_key, 2), number_of)]


def shared_out(key, own, number, rows, count, top, bound, skew):
    order = jax.random.permutation(key, count)
    crowded, common = portions_of(count, rows * top, bound, skew, True), portions_of(count, rows * top, bound, skew, False)
    places = jnp.arange(count)

    def named(lengths, rotation):
        used = int((lengths > 0).sum())
        fixed = max(1, used // 4)
        moved = fixed + (places - fixed + rotation * (used - fixed)) % max(1, count - fixed)
        return jnp.zeros((count,), jnp.int32).at[order[jnp.where(places < fixed, places, moved)]].set(jnp.asarray(lengths, jnp.int32))

    lengths = jnp.where(number % 4 == 0, named(crowded, number // 4), named(common, number - number // 4 - 1))
    mixed = jax.random.permutation(jax.random.fold_in(own, 3), count)
    donor, sink = mixed[0:count // 2 * 2:2], mixed[1:count // 2 * 2:2]
    slack = jnp.minimum(lengths[donor] - 1, bound - lengths[sink]) // 2
    slack = jnp.where((donor == order[0]) | (sink == order[0]) | (lengths[sink] == 0), 0, jnp.maximum(slack, 0))
    moved = jax.random.randint(jax.random.fold_in(own, 4), (count // 2,), 0, 1 << 20) % (slack + 1)
    lengths = lengths.at[donor].add(-moved).at[sink].add(moved)
    labels = jnp.searchsorted(jnp.cumsum(lengths), jnp.arange(rows * top), side="right").astype(jnp.int32)
    listing = labels.reshape(top, rows).T
    listing = listing[jax.random.permutation(jax.random.fold_in(own, 1), rows)]
    rotation = jax.random.randint(jax.random.fold_in(own, 2), (rows, 1), 0, top)
    return jnp.take_along_axis(listing, (jnp.arange(top)[None, :] + rotation) % top, axis=1)


def portions_of(count, total, bound, skew, full):
    portions = [(1 << 20) // math.isqrt(grade ** skew) + 1 for grade in range(1, count + 1)]
    largest = bound if full else min(bound, max(-(-total // count), total * portions[0] // sum(portions)))
    least = 1 if total - largest >= count - 1 else 0
    given, surplus = [largest] + [least] * (count - 1), total - largest - least * (count - 1)
    while surplus > 0:
        movable = [i for i in range(1, count) if given[i] < largest] or [i for i in range(1, count) if given[i] < bound]
        mass, remaining = sum([portions[i] for i in movable]), surplus
        for i in movable:
            addition = min(bound - given[i], max(1, remaining * portions[i] // mass), surplus)
            given[i] = given[i] + addition
            surplus = surplus - addition
    return np.array(given)


def scatter_about(key, shape, deviation, limit, split=(), kind=jnp.bfloat16):
    values = deviation * jax.random.normal(key, shape, jnp.float32)
    if split:
        values = values * levels(key, shape, split, -0.22, 0.18)
    return jnp.clip(values, -limit, limit).astype(kind)


def setup_inputs(seed: int = 0, part: int = 0) -> dict:
    seeds = jax.random.split(jax.random.key(seed), 12)
    part_keys = jax.random.split(jax.random.fold_in(seeds[11], part), 12)
    queries = draw_queries(jax.random.fold_in(jax.random.fold_in(seeds[11], part), 71), part)
    keys = draw_keys(jax.random.fold_in(jax.random.fold_in(seeds[11], part), 71), part)
    values = scatter_about(part_keys[2], (KEYS, KVH * HD), 1.0, 6.0, ((0, 16),))
    kv_lengths = uneven_parts(part_keys[3], N_CTX, KC * N_CTX // 2, KC, 2).astype(jnp.int32)
    stream = scatter_about(part_keys[4], (TOKENS, D), 1.0, 6.0, ((0, 16),))
    out_weight = scatter_about(seeds[5], (HEADS * HD, D), (HEADS * HD) ** -0.5, 0.125, ((0, 16),))
    routes_keys = jax.random.split(jax.random.fold_in(part_keys[6], 1), TOKENS // QD)
    routes_turns = jax.random.permutation(jax.random.fold_in(part_keys[6], 3), TOKENS // QD)
    routes = jax.vmap(lambda own, number: shared_out(jax.random.fold_in(part_keys[6], 2), own, number, QD, EXPERTS, TOP, CAP, 1))(routes_keys, routes_turns).reshape((TOKENS, TOP))
    gate_weights = jnp.clip(0.2 + 0.8 * jax.random.uniform(part_keys[7], (TOKENS, TOP), jnp.float32) ** levels(part_keys[7], (TOKENS, TOP), ((0, 16),), -0.2, 0.2), 0.2, 1.0)
    expert_gate = scatter_about(seeds[8], (EXPERTS, D, FFE), D ** -0.5, 0.125, ((0, 16),))
    expert_up = scatter_about(seeds[9], (EXPERTS, D, FFE), D ** -0.5, 0.125, ((0, 16),))
    expert_down = scatter_about(seeds[10], (EXPERTS, FFE, D), FFE ** -0.5, 0.21875, ((0, 16),))
    return dict(queries=queries, keys=keys, values=values, kv_lengths=kv_lengths, stream=stream, out_weight=out_weight, routes=routes, gate_weights=gate_weights, expert_gate=expert_gate, expert_up=expert_up, expert_down=expert_down)


def shard_part(block_q, key_rows, value_rows, length):
    grouped = block_q.astype(jnp.float32).reshape(QD, KVH, HEADS // KVH, HD)
    key_heads = key_rows.astype(jnp.float32).reshape(KC, KVH, HD)
    value_heads = value_rows.astype(jnp.float32).reshape(KC, KVH, HD)
    scores = jnp.einsum('qkgd,ckd->kgqc', grouped, key_heads) * HD ** (-0.5)
    valid_rows = jnp.arange(KC, dtype=jnp.int32) < length
    scores = jnp.where(valid_rows, scores, -1e+30)
    highest = lax.optimization_barrier(jnp.max(scores, axis=-1))
    weights = jnp.where(valid_rows, jnp.exp(scores - highest[..., None]), 0.0)
    totals = lax.optimization_barrier(jnp.sum(weights, axis=-1))
    rounded = lax.optimization_barrier(weights.astype(jnp.bfloat16)).astype(jnp.float32)
    part_out = jnp.einsum('kgqc,ckd->qkgd', rounded, value_heads)
    return (part_out, highest, totals)

def reference(queries, keys, values, kv_lengths, stream, out_weight, routes, gate_weights, expert_gate, expert_up, expert_down):
    key_width = keys.shape[1]
    padded_keys = jnp.concatenate([jnp.zeros(((STOPS - 1) * KC, key_width), keys.dtype), keys], axis=0)
    padded_values = jnp.concatenate([jnp.zeros(((STOPS - 1) * KC, key_width), values.dtype), values], axis=0)
    padded_lengths = jnp.concatenate([jnp.zeros((STOPS - 1,), jnp.int32), kv_lengths.astype(jnp.int32)])

    def attend_block(block_index):
        block_q = lax.dynamic_slice_in_dim(queries, (block_index * QD).astype(jnp.int32), QD, 0)
        key_window = lax.dynamic_slice_in_dim(padded_keys, (block_index * KC).astype(jnp.int32), STOPS * KC, 0)
        value_window = lax.dynamic_slice_in_dim(padded_values, (block_index * KC).astype(jnp.int32), STOPS * KC, 0)
        length_window = lax.dynamic_slice_in_dim(padded_lengths, block_index.astype(jnp.int32), STOPS, 0)
        outs_list = []
        maxima_list = []
        sums_list = []
        for station in range(STOPS):
            part_out, part_max, part_sum = shard_part(block_q, key_window[station * KC:(station + 1) * KC], value_window[station * KC:(station + 1) * KC], length_window[station])
            outs_list.append(part_out)
            maxima_list.append(part_max)
            sums_list.append(part_sum)
        maxima = jnp.stack(maxima_list)
        highest = lax.optimization_barrier(jnp.max(maxima, axis=0))
        factors = jnp.exp(maxima - highest)
        numerator = jnp.zeros_like(outs_list[0])
        denominator = jnp.zeros_like(sums_list[0])
        for station in range(STOPS):
            numerator = numerator + outs_list[station] * jnp.transpose(factors[station], (2, 0, 1))[..., None]
            denominator = denominator + factors[station] * sums_list[station]
        finished = numerator / jnp.transpose(denominator, (2, 0, 1))[..., None]
        return finished.reshape(QD, HEADS * HD).astype(jnp.bfloat16)
    attended = lax.map(attend_block, jnp.arange(N_CTX, dtype=jnp.int32)).reshape(TOKENS, HEADS * HD)
    projected = jnp.dot(attended, out_weight, preferred_element_type=jnp.float32)
    residual = (stream.astype(jnp.float32) + projected).astype(jnp.bfloat16)
    widened = lax.optimization_barrier(residual).astype(jnp.float32)
    normed = (widened * lax.rsqrt(lax.optimization_barrier(jnp.mean(widened * widened, axis=-1, keepdims=True)) + 1e-06)).astype(jnp.bfloat16)
    flat_routes = routes.reshape(-1).astype(jnp.int32)
    owner_row = jnp.arange(TOKENS * TOP, dtype=jnp.int32) // TOP
    flat_weights = gate_weights.reshape(-1)
    room_size = N_CTX * CAP

    def add_expert(expert, running):
        routed = flat_routes == expert
        within = jnp.cumsum(routed.astype(jnp.int32)) - 1
        target = jnp.where(routed, within, room_size).astype(jnp.int32)
        token_rows = jnp.zeros((room_size,), jnp.int32).at[target].set(owner_row, mode='drop')
        route_weight = jnp.zeros((room_size,), flat_weights.dtype).at[target].set(flat_weights, mode='drop')
        expert_in = normed[token_rows]
        gate_part = jnp.dot(expert_in, expert_gate[expert], preferred_element_type=jnp.float32)
        up_part = jnp.dot(expert_in, expert_up[expert], preferred_element_type=jnp.float32)
        hidden = (jax.nn.silu(gate_part) * up_part).astype(jnp.bfloat16)
        produced = jnp.dot(hidden, expert_down[expert], preferred_element_type=jnp.float32).astype(jnp.bfloat16)
        return running.at[token_rows].add(produced.astype(jnp.float32) * route_weight[:, None])
    mixture = lax.fori_loop(0, EXPERTS, add_expert, jnp.zeros((TOKENS, D), jnp.float32))
    layer_out = (widened + mixture).astype(jnp.bfloat16)
    return (attended, layer_out)
```

```python
import functools
import math

import jax
import jax.numpy as jnp
from jax import lax
from jax.experimental import pallas as pl
from jax.experimental.pallas import tpu as pltpu
from jax.sharding import PartitionSpec as P

HD = 128
STOPS = 8
CORES = 2


def from_behind(block, axis, distance):
    devices = range(lax.axis_size(axis))
    route = [(i - distance, i) for i in devices if i - distance in devices]
    return lax.ppermute(block, axis, route)


def attend_kernel(length_ref, q_ref, k_ref, v_ref, o_ref, bias_ref):
    stops = length_ref.shape[0]
    kv_rows = k_ref.shape[0] // stops

    @pl.when(pl.program_id(0) == 0)
    def _():
        row = lax.broadcasted_iota(jnp.int32, (1, kv_rows), 1)
        for stop in range(stops):
            bias_ref[:, stop * kv_rows : (stop + 1) * kv_rows] = jnp.where(
                row < length_ref[stop], 0.0, -1e30
            )

    scores = lax.dot_general(
        q_ref[...], k_ref[...], (((1,), (1,)), ((), ())), preferred_element_type=jnp.float32
    )
    scores = scores + bias_ref[...]
    highest = jnp.max(scores, axis=-1, keepdims=True)
    weights = jnp.exp2((scores - highest) * (HD ** (-0.5) * math.log2(math.e)))
    total = jnp.sum(weights, axis=-1, keepdims=True)
    out = jnp.dot(weights.astype(jnp.bfloat16), v_ref[...], preferred_element_type=jnp.float32)
    o_ref[...] = (out / total).astype(o_ref.dtype)


def attend(queries, window, lengths):
    rows, width = queries.shape
    kv_rows, kv_width = window.shape
    kv_heads = kv_width // (2 * HD)
    heads = width // HD
    group = heads // kv_heads
    return pl.pallas_call(
        attend_kernel,
        grid_spec=pltpu.PrefetchScalarGridSpec(
            num_scalar_prefetch=1,
            grid=(heads,),
            in_specs=[
                pl.BlockSpec((rows, HD), lambda h, n: (0, h)),
                pl.BlockSpec((kv_rows, HD), lambda h, n: (0, h // group)),
                pl.BlockSpec((kv_rows, HD), lambda h, n: (0, kv_heads + h // group)),
            ],
            out_specs=pl.BlockSpec((rows, HD), lambda h, n: (0, h)),
            scratch_shapes=[pltpu.VMEM((1, kv_rows), jnp.float32)],
        ),
        out_shape=jax.ShapeDtypeStruct((rows, width), jnp.bfloat16),
        cost_estimate=pl.CostEstimate(
            flops=4 * rows * width * kv_rows,
            transcendentals=rows * heads * kv_rows,
            bytes_accessed=2 * (2 * rows * width + kv_rows * kv_width),
        ),
        name="attend",
    )(lengths, queries, window, window)


def key_window(keys, values):
    window = jnp.concatenate([keys, values], axis=1)
    held = 1
    while held < STOPS:
        window = jnp.concatenate([window, from_behind(window, "ctx", held)], axis=0)
        held *= 2
    return window


def expert_kernel(count, chunks, *refs):
    x_refs = refs[:count]
    factor_ref = refs[count]
    own = refs[count + 1 : count + 4]
    other = refs[count + 4 : count + 7]
    o_refs = refs[count + 7 : 2 * count + 7]
    x_all, total = refs[2 * count + 7 :]
    step = pl.program_id(0)
    bounds = [0]
    for x_ref in x_refs:
        bounds.append(bounds[-1] + x_ref.shape[0])

    @pl.when(step == 0)
    def _():
        for x_ref, low, high in zip(x_refs, bounds, bounds[1:]):
            x_all[low:high, :] = x_ref[...]
        total[...] = jnp.zeros_like(total)

    def work(trio, column):
        gate_ref, up_ref, down_ref = trio
        x = x_all[...]
        gate = jnp.dot(x, gate_ref[0], preferred_element_type=jnp.float32)
        up = jnp.dot(x, up_ref[0], preferred_element_type=jnp.float32)
        hidden = gate / (1.0 + jnp.exp(-gate)) * up * factor_ref[:, column : column + 1]
        total[...] += jnp.dot(
            hidden.astype(jnp.bfloat16), down_ref[0], preferred_element_type=jnp.float32
        )

    pl.when(step < chunks)(lambda: work(own, 0))
    pl.when(step >= chunks)(lambda: work(other, 1))

    @pl.when(step == 2 * chunks - 1)
    def _():
        for o_ref, low, high in zip(o_refs, bounds, bounds[1:]):
            o_ref[...] = total[low:high, :].astype(o_ref.dtype)


def run_experts(blocks, factors, own, other):
    width = blocks[0].shape[1]
    hidden = own[0].shape[2]
    rows = sum(block.shape[0] for block in blocks)
    part = 256 if hidden % 256 == 0 else hidden
    chunks = hidden // part
    count = len(blocks)

    def held(i):
        return jnp.minimum(i, chunks - 1)

    def ahead(i):
        return jnp.maximum(i - chunks, 0)

    specs = [pl.BlockSpec(block.shape, lambda i: (0, 0)) for block in blocks]
    specs.append(pl.BlockSpec(factors.shape, lambda i: (0, 0)))
    for pick in (held, ahead):
        specs.append(pl.BlockSpec((1, width, part), lambda i, pick=pick: (0, 0, pick(i))))
        specs.append(pl.BlockSpec((1, width, part), lambda i, pick=pick: (0, 0, pick(i))))
        specs.append(pl.BlockSpec((1, part, width), lambda i, pick=pick: (0, pick(i), 0)))
    return pl.pallas_call(
        functools.partial(expert_kernel, count, chunks),
        grid=(2 * chunks,),
        in_specs=specs,
        out_specs=[pl.BlockSpec(block.shape, lambda i: (0, 0)) for block in blocks],
        out_shape=[jax.ShapeDtypeStruct(block.shape, jnp.bfloat16) for block in blocks],
        scratch_shapes=[
            pltpu.VMEM((rows, width), jnp.bfloat16),
            pltpu.VMEM((rows, width), jnp.float32),
        ],
        cost_estimate=pl.CostEstimate(
            flops=12 * rows * width * hidden,
            transcendentals=2 * rows * hidden,
            bytes_accessed=12 * width * hidden + 4 * rows * width,
        ),
        name="experts",
    )(*blocks, factors, *own, *other)


def project(attended, weight, stream):
    projected = jnp.dot(attended, weight, preferred_element_type=jnp.float32)
    residual = (stream.astype(jnp.float32) + projected).astype(jnp.bfloat16)
    widened = residual.astype(jnp.float32)
    normed = (
        widened * lax.rsqrt(jnp.mean(widened * widened, axis=-1, keepdims=True) + 1e-06)
    ).astype(jnp.bfloat16)
    return widened, normed


def chip_ring(devices):
    chips = devices // CORES
    return list(range(0, chips, 2)) + list(range(1, chips, 2))[::-1]


def ring_layer(
    queries, keys, values, kv_lengths, stream, out_weight, routes, gate_weights, own
):
    rows = queries.shape[0]
    devices = lax.axis_size("ctx")
    here = lax.axis_index("ctx")
    ring = chip_ring(devices)
    span = len(ring)
    half = span // 2

    def moved(block, distance):
        route = [
            (ring[i] * CORES + core, ring[(i + distance) % span] * CORES + core)
            for i in range(span)
            for core in range(CORES)
        ]
        return lax.ppermute(block, "ctx", route)

    swap = [(i, i ^ 1) for i in range(devices)]
    weight_all = lax.all_gather(out_weight, "ctx", axis=0, tiled=True)

    expert = jnp.arange(devices, dtype=jnp.int32)
    named = routes.T[None] == expert[:, None, None]
    factor = jnp.sum(jnp.where(named, gate_weights.T[None], 0.0), axis=1)
    swapped = factor.reshape(devices // 2, 2, rows)[:, ::-1].reshape(devices, rows)
    length_row = jnp.broadcast_to(kv_lengths.astype(jnp.float32), (devices, rows))
    notes = jnp.stack([factor, swapped, length_row, length_row], axis=1)
    notes = lax.all_to_all(notes, "ctx", split_axis=0, concat_axis=0, tiled=True)

    window = key_window(keys, values)
    behind = here - jnp.arange(STOPS, dtype=jnp.int32)
    lengths = jnp.sum(
        jnp.where(behind[:, None] == expert[None], notes[:, 2, 0][None], 0.0), axis=1
    ).astype(jnp.int32)

    other = [lax.ppermute(weight, "ctx", swap) for weight in own]

    attended = attend(queries, window, lengths)
    widened, normed = project(attended, weight_all, stream)

    place = [0] * span
    for i, chip in enumerate(ring):
        place[chip] = i
    ring_table = jnp.array(ring, jnp.int32)
    my_place = jnp.array(place, jnp.int32)[here // CORES]
    offsets = [0] + [s * k for k in range(1, half) for s in (-1, 1)] + [half]
    order = ring_table[(my_place + jnp.array(offsets, jnp.int32)) % span] * CORES + here % CORES
    picked = jnp.take(notes[:, :2], order, axis=0).transpose(0, 2, 1).reshape(-1, 2)

    def factors(first, number):
        return picked[first * rows : (first + number) * rows]

    cut = rows // 2
    forward, backward = [normed], [normed]
    for step in range(1, half):
        forward.append(moved(forward[-1], 1))
        backward.append(moved(backward[-1], -1))
    far_low = moved(forward[-1][:cut], 1)
    far_high = moved(backward[-1][cut:], -1)

    (home,) = run_experts([normed], factors(0, 1), own, other)
    from_forward, from_backward = [home], [home]
    for step in range(1, half):
        low, high = run_experts(
            [forward[step], backward[step]], factors(2 * step - 1, 2), own, other
        )
        from_forward.append(low)
        from_backward.append(high)
    far_low, far_high = run_experts(
        [far_low, far_high], factors(2 * half - 1, 1), own, other
    )

    def summed(a, b):
        return (a.astype(jnp.float32) + b.astype(jnp.float32)).astype(jnp.bfloat16)

    got_low = moved(far_low, -1)
    got_high = moved(far_high, 1)
    for step in range(half - 1, 0, -1):
        mine_low, mine_high = from_forward[step], from_backward[step]
        if step == half - 1:
            send_low = jnp.concatenate([summed(got_low, mine_low[:cut]), mine_low[cut:]])
            send_high = jnp.concatenate([mine_high[:cut], summed(got_high, mine_high[cut:])])
        else:
            send_low = summed(got_low, mine_low)
            send_high = summed(got_high, mine_high)
        got_low = moved(send_low, -1)
        got_high = moved(send_high, 1)
    mixture = (
        home.astype(jnp.float32) + got_low.astype(jnp.float32) + got_high.astype(jnp.float32)
    )
    return attended, (widened + mixture).astype(jnp.bfloat16)


def slot_layer(
    queries, keys, values, kv_lengths, stream, out_weight, routes, gate_weights, own
):
    expert_gate, expert_up, expert_down = own
    row_count = queries.shape[0]
    cycle_size = lax.axis_size("ctx")
    weight_all = lax.all_gather(out_weight, "ctx", axis=0, tiled=True)
    lengths = kv_lengths
    held = 1
    while held < STOPS:
        lengths = jnp.concatenate([lengths, from_behind(lengths, "ctx", held)])
        held *= 2
    attended = attend(queries, key_window(keys, values), lengths)
    widened, normed = project(attended, weight_all, stream)
    width = normed.shape[1]
    route_count = routes.shape[1]
    local_count = expert_gate.shape[0]
    expert_total = local_count * cycle_size
    capacity = slot_capacity(row_count, route_count, expert_total)
    flat_routes = routes.reshape(-1)
    one_hot = (flat_routes[:, None] == jnp.arange(expert_total, dtype=jnp.int32)[None, :]).astype(
        jnp.int32
    )
    earlier = jnp.cumsum(one_hot, axis=0) - one_hot
    slot_index = jnp.sum(earlier * one_hot, axis=1)
    slot_target = flat_routes * capacity + slot_index
    source_row = jnp.arange(row_count * route_count, dtype=jnp.int32) // route_count
    buffer_rows = jnp.zeros((expert_total * capacity,), jnp.int32).at[slot_target].set(source_row)
    buffer_live = jnp.zeros((expert_total * capacity,), jnp.bool_).at[slot_target].set(True)
    send_buffer = jnp.where(
        buffer_live[:, None], normed[buffer_rows], jnp.zeros((), jnp.bfloat16)
    ).reshape(expert_total, capacity, width)
    arrived = lax.all_to_all(send_buffer, "ctx", split_axis=0, concat_axis=0, tiled=True)
    by_source = arrived.reshape(cycle_size, local_count, capacity, width)
    gate_part = jnp.einsum(
        "nesd,edf->nesf", by_source, expert_gate, preferred_element_type=jnp.float32
    )
    up_part = jnp.einsum("nesd,edf->nesf", by_source, expert_up, preferred_element_type=jnp.float32)
    hidden = (jax.nn.silu(gate_part) * up_part).astype(jnp.bfloat16)
    produced = jnp.einsum(
        "nesf,efd->nesd", hidden, expert_down, preferred_element_type=jnp.float32
    ).astype(jnp.bfloat16)
    returned = lax.all_to_all(
        produced.reshape(cycle_size * local_count, capacity, width),
        "ctx",
        split_axis=0,
        concat_axis=0,
        tiled=True,
    )
    gathered = returned.reshape(expert_total * capacity, width)[slot_target].reshape(
        row_count, route_count, width
    )
    mixture = jnp.zeros((row_count, width), jnp.float32)
    for route in range(route_count):
        mixture = mixture + gate_weights[:, route : route + 1] * gathered[:, route].astype(
            jnp.float32
        )
    return attended, (widened + mixture).astype(jnp.bfloat16)


def slot_capacity(row_count, route_count, expert_total):
    return max(2, row_count * route_count * 9 // (8 * expert_total))


def shards(
    queries,
    keys,
    values,
    kv_lengths,
    stream,
    out_weight,
    routes,
    gate_weights,
    expert_gate,
    expert_up,
    expert_down,
):
    rows = queries.shape[0]
    devices = lax.axis_size("ctx")
    local_count = expert_gate.shape[0]
    capacity = slot_capacity(rows, routes.shape[1], local_count * devices)
    crowded = local_count == 1 and 4 * capacity > rows and devices % (2 * CORES) == 0
    layer = ring_layer if crowded else slot_layer
    return layer(
        queries,
        keys,
        values,
        kv_lengths,
        stream,
        out_weight,
        routes,
        gate_weights,
        (expert_gate, expert_up, expert_down),
    )


def solution(mesh):
    return jax.shard_map(
        shards,
        mesh=mesh,
        in_specs=(
            P(("groups", "ctx"), None),
            P(("groups", "ctx"), None),
            P(("groups", "ctx"), None),
            P(("groups", "ctx")),
            P(("groups", "ctx"), None),
            P("ctx", None),
            P(("groups", "ctx"), None),
            P(("groups", "ctx"), None),
            P("ctx", None, None),
            P("ctx", None, None),
            P("ctx", None, None),
        ),
        out_specs=(P(("groups", "ctx"), None), P(("groups", "ctx"), None)),
        check_vma=False,
    )
```

```python
import functools
import math

import jax
import jax.numpy as jnp
from jax import lax
from jax.experimental import pallas as pl
from jax.experimental.pallas import tpu as pltpu
from jax.sharding import PartitionSpec as P

HD = 128
STOPS = 8
CORES = 2


def from_behind(block, axis, distance):
    devices = range(lax.axis_size(axis))
    route = [(i - distance, i) for i in devices if i - distance in devices]
    return lax.ppermute(block, axis, route)


def attend_kernel(heads, length_ref, q_ref, k_ref, v_ref, o_ref, bias_ref):
    stops = length_ref.shape[0]
    kv_rows = k_ref.shape[0] // stops
    rows = q_ref.shape[0]

    @pl.when(pl.program_id(0) == 0)
    def _():
        row = lax.broadcasted_iota(jnp.int32, (1, kv_rows), 1)
        for stop in range(stops):
            bias_ref[:, stop * kv_rows : (stop + 1) * kv_rows] = jnp.where(
                row < length_ref[stop], 0.0, -1e30
            )

    stacked = jnp.concatenate([q_ref[:, h * HD : (h + 1) * HD] for h in range(heads)], axis=0)
    scores = lax.dot_general(
        stacked, k_ref[...], (((1,), (1,)), ((), ())), preferred_element_type=jnp.float32
    )
    scores = scores * (HD ** (-0.5) * math.log2(math.e)) + bias_ref[...]
    highest = jnp.max(scores, axis=-1, keepdims=True)
    weights = jnp.exp2(scores - highest)
    total = jnp.sum(weights, axis=-1, keepdims=True)
    out = jnp.dot(weights.astype(jnp.bfloat16), v_ref[...], preferred_element_type=jnp.float32)
    out = (out / total).astype(o_ref.dtype)
    for h in range(heads):
        o_ref[:, h * HD : (h + 1) * HD] = out[h * rows : (h + 1) * rows]


def attend(queries, window, lengths):
    rows, width = queries.shape
    kv_rows, kv_width = window.shape
    kv_heads = kv_width // (2 * HD)
    heads = width // HD
    pair = 2 if heads // kv_heads % 2 == 0 else 1
    group = heads // kv_heads // pair
    return pl.pallas_call(
        functools.partial(attend_kernel, pair),
        grid_spec=pltpu.PrefetchScalarGridSpec(
            num_scalar_prefetch=1,
            grid=(heads // pair,),
            in_specs=[
                pl.BlockSpec((rows, pair * HD), lambda h, n: (0, h)),
                pl.BlockSpec((kv_rows, HD), lambda h, n: (0, h // group)),
                pl.BlockSpec((kv_rows, HD), lambda h, n: (0, kv_heads + h // group)),
            ],
            out_specs=pl.BlockSpec((rows, pair * HD), lambda h, n: (0, h)),
            scratch_shapes=[pltpu.VMEM((1, kv_rows), jnp.float32)],
        ),
        out_shape=jax.ShapeDtypeStruct((rows, width), jnp.bfloat16),
        cost_estimate=pl.CostEstimate(
            flops=4 * rows * width * kv_rows,
            transcendentals=rows * heads * kv_rows,
            bytes_accessed=2 * (2 * rows * width + kv_rows * kv_width),
        ),
        name="attend",
    )(lengths, queries, window, window)


def key_window(keys, values):
    window = jnp.concatenate([keys, values], axis=1)
    held = 1
    while held < STOPS:
        window = jnp.concatenate([window, from_behind(window, "ctx", held)], axis=0)
        held *= 2
    return window


def expert_kernel(count, *refs):
    x_refs = refs[:count]
    factor_ref = refs[count]
    trios = (refs[count + 1 : count + 4], refs[count + 4 : count + 7])
    o_refs = refs[count + 7 :]
    x = jnp.concatenate([x_ref[...] for x_ref in x_refs], axis=0)
    total = None
    for column, (gate_ref, up_ref, down_ref) in enumerate(trios):
        gate = jnp.dot(x, gate_ref[0], preferred_element_type=jnp.float32)
        up = jnp.dot(x, up_ref[0], preferred_element_type=jnp.float32)
        hidden = gate / (1.0 + jnp.exp(-gate)) * up * factor_ref[:, column : column + 1]
        part = jnp.dot(hidden.astype(jnp.bfloat16), down_ref[0], preferred_element_type=jnp.float32)
        total = part if total is None else total + part
    low = 0
    for o_ref in o_refs:
        high = low + o_ref.shape[0]
        o_ref[...] = total[low:high].astype(o_ref.dtype)
        low = high


def run_experts(blocks, factors, own, other):
    width = blocks[0].shape[1]
    hidden = own[0].shape[2]
    rows = sum(block.shape[0] for block in blocks)
    count = len(blocks)
    held = pl.BlockSpec(memory_space=pltpu.VMEM)
    return pl.pallas_call(
        functools.partial(expert_kernel, count),
        in_specs=[held] * (count + 7),
        out_specs=[held] * count,
        out_shape=[jax.ShapeDtypeStruct(block.shape, jnp.bfloat16) for block in blocks],
        compiler_params=pltpu.CompilerParams(vmem_limit_bytes=40 * 1024 * 1024),
        cost_estimate=pl.CostEstimate(
            flops=12 * rows * width * hidden,
            transcendentals=2 * rows * hidden,
            bytes_accessed=12 * width * hidden + 4 * rows * width,
        ),
        name="experts",
    )(*blocks, factors, *own, *other)


def project(attended, weight, stream):
    projected = jnp.dot(attended, weight, preferred_element_type=jnp.float32)
    residual = (stream.astype(jnp.float32) + projected).astype(jnp.bfloat16)
    widened = residual.astype(jnp.float32)
    normed = (
        widened * lax.rsqrt(jnp.mean(widened * widened, axis=-1, keepdims=True) + 1e-06)
    ).astype(jnp.bfloat16)
    return widened, normed


def chip_ring(devices):
    chips = devices // CORES
    return list(range(0, chips, 2)) + list(range(1, chips, 2))[::-1]


def near_window(keys, values, first_after):
    devices = lax.axis_size("ctx")
    here = lax.axis_index("ctx")
    core, side = here % 2, here // 2 % 2
    rows = keys.shape[0]
    flip = [[(i, i ^ bit) for i in range(devices)] for bit in (1, 2)]
    mine = jnp.concatenate([keys, values], axis=1)
    second = from_behind(mine, "ctx", 4)
    second, first_after = lax.optimization_barrier((second, first_after))
    fourth = from_behind(second, "ctx", 4)
    crossing = jnp.where(
        side == 0,
        jnp.concatenate([mine, second], axis=0),
        jnp.concatenate([second, fourth], axis=0),
    )
    crossed = lax.ppermute(crossing, "ctx", flip[1])
    shared = jnp.concatenate([jnp.where(core == 0, mine, fourth), second, crossed], axis=0)
    got = lax.ppermute(shared, "ctx", flip[0])
    window = jnp.concatenate([mine, second, crossed, got], axis=0)
    near = [0, 4, 2, 6]
    other = jnp.where(core == 1, jnp.array([1, 5, 3, 7]), jnp.array([7, 3, 1, 5]))
    return window, here - jnp.concatenate([jnp.array(near), other]), first_after


def ring_layer(
    queries, keys, values, kv_lengths, stream, out_weight, routes, gate_weights, own
):
    rows = queries.shape[0]
    devices = lax.axis_size("ctx")
    here = lax.axis_index("ctx")
    ring = chip_ring(devices)
    span = len(ring)
    half = span // 2

    def moved(block, distance):
        route = [
            (ring[i] * CORES + core, ring[(i + distance) % span] * CORES + core)
            for i in range(span)
            for core in range(CORES)
        ]
        return lax.ppermute(block, "ctx", route)

    swap = [(i, i ^ 1) for i in range(devices)]
    weight_all = lax.all_gather(out_weight, "ctx", axis=0, tiled=True)

    expert = jnp.arange(devices, dtype=jnp.int32)
    named = routes.T[None] == expert[:, None, None]
    factor = jnp.sum(jnp.where(named, gate_weights.T[None], 0.0), axis=1)
    swapped = factor.reshape(devices // 2, 2, rows)[:, ::-1].reshape(devices, rows)
    length_row = jnp.broadcast_to(kv_lengths.astype(jnp.float32), (devices, rows))
    notes = jnp.stack([factor, swapped, length_row, length_row], axis=1)
    notes = lax.all_to_all(notes, "ctx", split_axis=0, concat_axis=0, tiled=True)

    window, shard_ids, notes = near_window(keys, values, notes)
    lengths = jnp.sum(
        jnp.where(shard_ids[:, None] == expert[None], notes[:, 2, 0][None], 0.0), axis=1
    ).astype(jnp.int32)

    place = [0] * span
    for i, chip in enumerate(ring):
        place[chip] = i
    ring_table = jnp.array(ring, jnp.int32)
    my_place = jnp.array(place, jnp.int32)[here // CORES]
    offsets = [0] + [s * k for k in range(1, half) for s in (-1, 1)] + [half]
    order = ring_table[(my_place + jnp.array(offsets, jnp.int32)) % span] * CORES + here % CORES
    picked = jnp.take(notes[:, :2], order, axis=0).transpose(0, 2, 1).reshape(-1, 2)

    window, picked, *late = lax.optimization_barrier((window, picked, *own))
    other = [lax.ppermute(weight, "ctx", swap) for weight in late]
    attended = attend(queries, window, lengths)
    own = [pltpu.with_memory_space_constraint(weight, pltpu.VMEM) for weight in own]
    other = [pltpu.with_memory_space_constraint(weight, pltpu.VMEM) for weight in other]
    widened, normed = project(attended, weight_all, stream)

    def factors(first, number):
        return picked[first * rows : (first + number) * rows]

    cut = rows // 2
    (home,) = run_experts([normed], factors(0, 1), own, other)
    ahead, back = normed, normed
    done = [home]
    sums = []
    for step in range(1, half):
        ahead, back = moved(ahead, 1), moved(back, -1)
        ahead, back, *done = lax.optimization_barrier((ahead, back, *done))
        sums.append(done)
        done = run_experts([ahead, back], factors(2 * step - 1, 2), own, other)
    far_low, far_high = moved(ahead[:cut], 1), moved(back[cut:], -1)
    far_low, far_high, *done = lax.optimization_barrier((far_low, far_high, *done))
    sums.append(done)
    far_low, far_high = run_experts(
        [far_low, far_high], factors(2 * half - 1, 1), own, other
    )

    def summed(a, b):
        return (a.astype(jnp.float32) + b.astype(jnp.float32)).astype(jnp.bfloat16)

    got_low, got_high = moved(far_low, -1), moved(far_high, 1)
    for step in range(half - 1, 0, -1):
        mine_low, mine_high = sums[step]
        if step == half - 1:
            send_low = jnp.concatenate([summed(got_low, mine_low[:cut]), mine_low[cut:]])
            send_high = jnp.concatenate([mine_high[:cut], summed(got_high, mine_high[cut:])])
        else:
            send_low = summed(got_low, mine_low)
            send_high = summed(got_high, mine_high)
        got_low, got_high = moved(send_low, -1), moved(send_high, 1)
    (home,) = sums[0]
    mixture = (
        home.astype(jnp.float32) + got_low.astype(jnp.float32) + got_high.astype(jnp.float32)
    )
    return attended, (widened + mixture).astype(jnp.bfloat16)


def slot_layer(
    queries, keys, values, kv_lengths, stream, out_weight, routes, gate_weights, own
):
    expert_gate, expert_up, expert_down = own
    row_count = queries.shape[0]
    cycle_size = lax.axis_size("ctx")
    weight_all = lax.all_gather(out_weight, "ctx", axis=0, tiled=True)
    lengths = kv_lengths
    held = 1
    while held < STOPS:
        lengths = jnp.concatenate([lengths, from_behind(lengths, "ctx", held)])
        held *= 2
    attended = attend(queries, key_window(keys, values), lengths)
    widened, normed = project(attended, weight_all, stream)
    width = normed.shape[1]
    route_count = routes.shape[1]
    local_count = expert_gate.shape[0]
    expert_total = local_count * cycle_size
    capacity = slot_capacity(row_count, route_count, expert_total)
    flat_routes = routes.reshape(-1)
    one_hot = (flat_routes[:, None] == jnp.arange(expert_total, dtype=jnp.int32)[None, :]).astype(
        jnp.int32
    )
    earlier = jnp.cumsum(one_hot, axis=0) - one_hot
    slot_index = jnp.sum(earlier * one_hot, axis=1)
    slot_target = flat_routes * capacity + slot_index
    source_row = jnp.arange(row_count * route_count, dtype=jnp.int32) // route_count
    buffer_rows = jnp.zeros((expert_total * capacity,), jnp.int32).at[slot_target].set(source_row)
    buffer_live = jnp.zeros((expert_total * capacity,), jnp.bool_).at[slot_target].set(True)
    send_buffer = jnp.where(
        buffer_live[:, None], normed[buffer_rows], jnp.zeros((), jnp.bfloat16)
    ).reshape(expert_total, capacity, width)
    arrived = lax.all_to_all(send_buffer, "ctx", split_axis=0, concat_axis=0, tiled=True)
    by_source = arrived.reshape(cycle_size, local_count, capacity, width)
    gate_part = jnp.einsum(
        "nesd,edf->nesf", by_source, expert_gate, preferred_element_type=jnp.float32
    )
    up_part = jnp.einsum("nesd,edf->nesf", by_source, expert_up, preferred_element_type=jnp.float32)
    hidden = (jax.nn.silu(gate_part) * up_part).astype(jnp.bfloat16)
    produced = jnp.einsum(
        "nesf,efd->nesd", hidden, expert_down, preferred_element_type=jnp.float32
    ).astype(jnp.bfloat16)
    returned = lax.all_to_all(
        produced.reshape(cycle_size * local_count, capacity, width),
        "ctx",
        split_axis=0,
        concat_axis=0,
        tiled=True,
    )
    gathered = returned.reshape(expert_total * capacity, width)[slot_target].reshape(
        row_count, route_count, width
    )
    mixture = jnp.zeros((row_count, width), jnp.float32)
    for route in range(route_count):
        mixture = mixture + gate_weights[:, route : route + 1] * gathered[:, route].astype(
            jnp.float32
        )
    return attended, (widened + mixture).astype(jnp.bfloat16)


def slot_capacity(row_count, route_count, expert_total):
    return max(2, row_count * route_count * 9 // (8 * expert_total))


def shards(
    queries,
    keys,
    values,
    kv_lengths,
    stream,
    out_weight,
    routes,
    gate_weights,
    expert_gate,
    expert_up,
    expert_down,
):
    rows = queries.shape[0]
    devices = lax.axis_size("ctx")
    local_count = expert_gate.shape[0]
    capacity = slot_capacity(rows, routes.shape[1], local_count * devices)
    crowded = local_count == 1 and 4 * capacity > rows and devices % (2 * CORES) == 0
    layer = ring_layer if crowded else slot_layer
    return layer(
        queries,
        keys,
        values,
        kv_lengths,
        stream,
        out_weight,
        routes,
        gate_weights,
        (expert_gate, expert_up, expert_down),
    )


def solution(mesh):
    return jax.shard_map(
        shards,
        mesh=mesh,
        in_specs=(
            P(("groups", "ctx"), None),
            P(("groups", "ctx"), None),
            P(("groups", "ctx"), None),
            P(("groups", "ctx")),
            P(("groups", "ctx"), None),
            P("ctx", None),
            P(("groups", "ctx"), None),
            P(("groups", "ctx"), None),
            P("ctx", None, None),
            P("ctx", None, None),
            P("ctx", None, None),
        ),
        out_specs=(P(("groups", "ctx"), None), P(("groups", "ctx"), None)),
        check_vma=False,
    )
```

```python
import functools
import math

import jax
import jax.numpy as jnp
from jax import lax
from jax.experimental import pallas as pl
from jax.experimental.pallas import tpu as pltpu
from jax.sharding import PartitionSpec as P


HD = 128
STOPS = 8
CORES = 2
DEAD = 1e30


def from_behind(block, axis, distance):
    devices = range(lax.axis_size(axis))
    route = [(i - distance, i) for i in devices if i - distance in devices]
    return lax.ppermute(block, axis, route)


def attend_kernel(heads, parts, length_ref, core_ref, q_ref, *refs):
    k_refs, v_refs, rest = refs[:parts], refs[parts : 2 * parts], refs[2 * parts :]
    o_ref, split_refs, bias_ref = rest[0], rest[1:-1], rest[-1]
    stops = length_ref.shape[0]
    kv_rows = bias_ref.shape[1] // stops
    rows = q_ref.shape[0]

    @pl.when(pl.program_id(0) == 0)
    def _():
        if split_refs:
            first_lane = lax.broadcasted_iota(jnp.int32, (16, HD), 1) == 0
            marks = lax.dot_general(
                first_lane.astype(jnp.float32).astype(jnp.bfloat16),
                jnp.concatenate([v_ref[...] for v_ref in v_refs], axis=0),
                (((1,), (1,)), ((), ())),
                preferred_element_type=jnp.float32,
            )[:1]
        row = lax.broadcasted_iota(jnp.int32, (1, kv_rows), 1)
        for stop in range(stops):
            part = slice(stop * kv_rows, (stop + 1) * kv_rows)
            if split_refs:
                dead = (marks[:, part] > DEAD / 2) | (row < kv_rows * (1 - length_ref[stop]))
            else:
                dead = row >= length_ref[stop]
            bias_ref[:, part] = jnp.where(dead, -1e30, 0.0)

    stacked = jnp.concatenate([q_ref[:, h * HD : (h + 1) * HD] for h in range(heads)], axis=0)
    scores = lax.dot_general(
        stacked,
        jnp.concatenate([k_ref[...] for k_ref in k_refs], axis=0),
        (((1,), (1,)), ((), ())),
        preferred_element_type=jnp.float32,
    )
    scores = scores * (HD ** (-0.5) * math.log2(math.e)) + bias_ref[...]
    highest = jnp.max(scores, axis=-1, keepdims=True)
    weights = jnp.exp2(scores - highest)
    total = jnp.sum(weights, axis=-1, keepdims=True)
    out = jnp.dot(
        weights.astype(jnp.bfloat16),
        jnp.concatenate([v_ref[...] for v_ref in v_refs], axis=0),
        preferred_element_type=jnp.float32,
    )
    out = (out / total).astype(o_ref.dtype)
    for h in range(heads):
        o_ref[:, h * HD : (h + 1) * HD] = out[h * rows : (h + 1) * rows]
    if split_refs:
        mine_ref, theirs_ref = split_refs
        first = core_ref[0] == 0
        mine_ref[...] = jnp.where(first, out[:rows], out[rows:])
        theirs_ref[...] = jnp.where(first, out[rows:], out[:rows])


def attend(queries, windows, lengths, core=None):
    rows, width = queries.shape
    kv_rows = sum(window.shape[0] for window in windows)
    kv_width = windows[0].shape[1]
    kv_heads = kv_width // (2 * HD)
    heads = width // HD
    pair = 2 if heads // kv_heads % 2 == 0 else 1
    group = heads // kv_heads // pair
    split = core is not None
    number = core if split else jnp.zeros((), jnp.int32)
    outs = [jax.ShapeDtypeStruct((rows, width), jnp.bfloat16)]
    outs += [jax.ShapeDtypeStruct((rows, width // 2), jnp.bfloat16)] * (2 * split)
    out_specs = [pl.BlockSpec((rows, pair * HD), lambda h, n, c: (0, h))]
    out_specs += [pl.BlockSpec((rows, HD), lambda h, n, c: (0, h))] * (2 * split)
    specs = [pl.BlockSpec((rows, pair * HD), lambda h, n, c: (0, h))]
    for first in (0, kv_heads):
        for window in windows:
            specs.append(
                pl.BlockSpec(
                    (window.shape[0], HD), lambda h, n, c, first=first: (0, first + h // group)
                )
            )
    return pl.pallas_call(
        functools.partial(attend_kernel, pair, len(windows)),
        grid_spec=pltpu.PrefetchScalarGridSpec(
            num_scalar_prefetch=2,
            grid=(heads // pair,),
            in_specs=specs,
            out_specs=out_specs,
            scratch_shapes=[pltpu.VMEM((1, kv_rows), jnp.float32)],
        ),
        out_shape=outs,
        compiler_params=pltpu.CompilerParams(vmem_limit_bytes=20 * 1024 * 1024),
        cost_estimate=pl.CostEstimate(
            flops=4 * rows * width * kv_rows,
            transcendentals=rows * heads * kv_rows,
            bytes_accessed=2 * (2 * rows * width + kv_rows * kv_width),
        ),
        name="attend",
    )(lengths, number.reshape(1), queries, *windows, *windows)


def key_window(keys, values):
    window = jnp.concatenate([keys, values], axis=1)
    held = 1
    while held < STOPS:
        window = jnp.concatenate([window, from_behind(window, "ctx", held)], axis=0)
        held *= 2
    return window


def expert_kernel(count, *refs):
    x_refs = refs[:count]
    factor_ref = refs[count]
    trios = (refs[count + 1 : count + 4], refs[count + 4 : count + 7])
    o_refs = refs[count + 7 :]
    x = jnp.concatenate([x_ref[...] for x_ref in x_refs], axis=0)
    total = None
    for column, (gate_ref, up_ref, down_ref) in enumerate(trios):
        gate = jnp.dot(x, gate_ref[0], preferred_element_type=jnp.float32)
        up = jnp.dot(x, up_ref[0], preferred_element_type=jnp.float32)
        hidden = gate / (1.0 + jnp.exp(-gate)) * up * factor_ref[:, column : column + 1]
        part = jnp.dot(hidden.astype(jnp.bfloat16), down_ref[0], preferred_element_type=jnp.float32)
        total = part if total is None else total + part
    low = 0
    for o_ref in o_refs:
        high = low + o_ref.shape[0]
        o_ref[...] = total[low:high].astype(o_ref.dtype)
        low = high


def run_experts(blocks, factors, own, other):
    width = blocks[0].shape[1]
    hidden = own[0].shape[2]
    rows = sum(block.shape[0] for block in blocks)
    count = len(blocks)
    held = pl.BlockSpec(memory_space=pltpu.VMEM)
    return pl.pallas_call(
        functools.partial(expert_kernel, count),
        in_specs=[held] * (count + 7),
        out_specs=[held] * count,
        out_shape=[jax.ShapeDtypeStruct(block.shape, jnp.bfloat16) for block in blocks],
        compiler_params=pltpu.CompilerParams(vmem_limit_bytes=20 * 1024 * 1024),
        cost_estimate=pl.CostEstimate(
            flops=12 * rows * width * hidden,
            transcendentals=2 * rows * hidden,
            bytes_accessed=12 * width * hidden + 4 * rows * width,
        ),
        name="experts",
    )(*blocks, factors, *own, *other)


def project(attended, weight, stream):
    projected = jnp.dot(attended, weight, preferred_element_type=jnp.float32)
    residual = (stream.astype(jnp.float32) + projected).astype(jnp.bfloat16)
    widened = residual.astype(jnp.float32)
    normed = (
        widened * lax.rsqrt(jnp.mean(widened * widened, axis=-1, keepdims=True) + 1e-06)
    ).astype(jnp.bfloat16)
    return widened, normed


def project_kernel(order_ref, mine_ref, got_ref, *refs):
    *pieces, keep_ref, give_ref = refs
    rows = mine_ref.shape[0]
    total = None
    for index in range(0, len(pieces), 2):
        columns = []
        for place in (index, index + 1):
            low = pl.multiple_of(order_ref[place] * HD, HD)
            columns.append(
                jnp.concatenate([mine_ref[:, pl.ds(low, HD)], got_ref[:, pl.ds(low, HD)]], axis=0)
            )
        part = jnp.dot(
            jnp.concatenate(columns, axis=1),
            jnp.concatenate([pieces[index][...], pieces[index + 1][...]], axis=0),
            preferred_element_type=jnp.float32,
        )
        total = part if total is None else total + part
    keep_ref[...] = total[:rows]
    give_ref[...] = total[rows:]


def project_pieces(mine, got, pieces, order):
    rows = mine.shape[0]
    width = pieces[0].shape[1]
    part = 512 if width % 512 == 0 else width
    whole = pl.BlockSpec(mine.shape, lambda i, n: (0, 0))
    wide = pl.BlockSpec((rows, part), lambda i, n: (0, i))
    like = jax.ShapeDtypeStruct((rows, width), jnp.float32)
    return pl.pallas_call(
        project_kernel,
        grid_spec=pltpu.PrefetchScalarGridSpec(
            num_scalar_prefetch=1,
            grid=(width // part,),
            in_specs=[whole, whole]
            + [pl.BlockSpec((piece.shape[0], part), lambda i, n: (0, i)) for piece in pieces],
            out_specs=[wide, wide],
        ),
        out_shape=[like, like],
        compiler_params=pltpu.CompilerParams(vmem_limit_bytes=20 * 1024 * 1024),
        cost_estimate=pl.CostEstimate(
            flops=4 * rows * width * mine.shape[1],
            transcendentals=0,
            bytes_accessed=2 * mine.shape[1] * width + 8 * rows * width,
        ),
        name="project",
    )(order, mine, got, *pieces)


def norm_kernel(stream_ref, keep_ref, got_ref, residual_ref, normed_ref):
    total = stream_ref[...].astype(jnp.float32) + keep_ref[...] + got_ref[...]
    residual = total.astype(jnp.bfloat16)
    residual_ref[...] = residual
    widened = residual.astype(jnp.float32)
    square = jnp.mean(widened * widened, axis=-1, keepdims=True)
    normed_ref[...] = (widened * lax.rsqrt(square + 1e-06)).astype(jnp.bfloat16)


def add_norm(stream, keep, got):
    rows, width = stream.shape
    like = jax.ShapeDtypeStruct(stream.shape, jnp.bfloat16)
    part = rows // 4 if rows % 64 == 0 else rows
    held = pl.BlockSpec((part, width), lambda i: (i, 0))
    return pl.pallas_call(
        norm_kernel,
        grid=(rows // part,),
        in_specs=[held] * 3,
        out_specs=[held, held],
        out_shape=[like, like],
        compiler_params=pltpu.CompilerParams(vmem_limit_bytes=20 * 1024 * 1024),
        name="add_norm",
    )(stream, keep, got)


def chip_ring(devices):
    chips = devices // CORES
    return list(range(0, chips, 2)) + list(range(1, chips, 2))[::-1]


def ring_layer(
    queries, keys, values, kv_lengths, stream, out_weight, routes, gate_weights, own
):
    rows = queries.shape[0]
    devices = lax.axis_size("ctx")
    here = lax.axis_index("ctx")
    ring = chip_ring(devices)
    span = len(ring)
    half = span // 2
    core, side = here % 2, here // 2 % 2
    flip = [[(i, i ^ bit) for i in range(devices)] for bit in (1, 2)]

    def moved(block, distance):
        route = [
            (ring[i] * CORES + c, ring[(i + distance) % span] * CORES + c)
            for i in range(span)
            for c in range(CORES)
        ]
        return lax.ppermute(block, "ctx", route)

    def swapped(block):
        return lax.ppermute(block, "ctx", flip[0])

    def far_memory(array):
        return pltpu.with_memory_space_constraint(array, pltpu.HBM)

    def near_memory(arrays):
        return [pltpu.with_memory_space_constraint(array, pltpu.VMEM) for array in arrays]

    chip = here // CORES
    my_place = jnp.where(chip % 2 == 0, chip // 2, span - 1 - chip // 2)
    offsets = [0] + [s * k for k in range(1, half) for s in (-1, 1)] + [half]
    places = (my_place + jnp.array(offsets, jnp.int32)) % span
    chips = jnp.where(places < half, 2 * places, 2 * (span - 1 - places) + 1)
    order = chips * CORES + core
    near = jnp.array([0, 4, 2, 6, 1, 5, 3, 7], jnp.int32)
    far = jnp.array([0, 4, 2, 6, 7, 3, 1, 5], jnp.int32)
    reached = (here - jnp.where(core == 1, near, far) >= 0).astype(jnp.int32)

    kv_rows = keys.shape[0]
    live = jnp.arange(kv_rows, dtype=jnp.int32)[:, None] < kv_lengths[0]
    expert = jnp.arange(devices, dtype=jnp.int32)
    named = routes.T[None] == expert[:, None, None]
    factor = jnp.sum(jnp.where(named, gate_weights.T[None], 0.0), axis=1)
    factor_swap = factor.reshape(devices // 2, 2, rows)[:, ::-1].reshape(devices, rows)
    notes = jnp.stack([factor, factor_swap], axis=1)

    ahead, back = moved(out_weight, 1), moved(out_weight, -1)
    mine = jnp.concatenate([keys, jnp.where(live, values, DEAD).astype(values.dtype)], axis=1)
    second = from_behind(mine, "ctx", 4)
    pieces = [out_weight]
    fourth = crossed = crossed_far = None
    for step in range(2, half + 1):
        if step == 2:
            second, ahead, back, notes, *late = lax.optimization_barrier(
                (second, ahead, back, notes, *own)
            )
            notes = lax.all_to_all(notes, "ctx", split_axis=0, concat_axis=0, tiled=True)
            fourth = from_behind(second, "ctx", 4)
            crossed = lax.ppermute(jnp.where(side == 0, mine, second), "ctx", flip[1])
            other = [swapped(weight) for weight in late]
        elif step == 3:
            fourth, crossed, ahead, back, notes = lax.optimization_barrier(
                (fourth, crossed, ahead, back, notes)
            )
            crossed_far = lax.ppermute(jnp.where(side == 0, second, fourth), "ctx", flip[1])
        else:
            ahead, back = lax.optimization_barrier((ahead, back))
        pieces += [far_memory(ahead), far_memory(back)]
        if step < half:
            ahead, back = moved(ahead, 1), moved(back, -1)
    if crossed_far is None:
        crossed_far = lax.ppermute(jnp.where(side == 0, second, fourth), "ctx", flip[1])
    windows = [mine, second, crossed, crossed_far]
    shared = [jnp.where(core == 0, mine, fourth), second, crossed, crossed_far]
    windows += [swapped(window) for window in shared]
    ahead, notes, *windows = lax.optimization_barrier((ahead, notes, *windows))
    last = moved(ahead, 1)
    pieces.append(far_memory(last))
    attended, kept, given = attend(queries, windows, reached, core)
    got = swapped(given)
    chosen = (order[:, None] == expert[None])[:, :, None, None]
    picked = jnp.sum(jnp.where(chosen, notes[None], 0.0), axis=1)
    picked = picked.transpose(0, 2, 1).reshape(-1, 2)

    own, other = near_memory(own), near_memory(other)
    keep, give = project_pieces(kept, got, pieces, chips)
    residual, normed = add_norm(stream, keep, swapped(give))

    def factors(first, number):
        return picked[first * rows : (first + number) * rows]

    cut = rows // 2
    (home,) = run_experts([normed], factors(0, 1), own, other)
    ahead, back = normed, normed
    done = [home]
    sums = []
    for step in range(1, half):
        ahead, back = moved(ahead, 1), moved(back, -1)
        ahead, back, *done = lax.optimization_barrier((ahead, back, *done))
        sums.append(done)
        done = run_experts([ahead, back], factors(2 * step - 1, 2), own, other)
    far_low, far_high = moved(ahead[:cut], 1), moved(back[cut:], -1)
    far_low, far_high, *done = lax.optimization_barrier((far_low, far_high, *done))
    sums.append(done)
    far_low, far_high = run_experts(
        [far_low, far_high], factors(2 * half - 1, 1), own, other
    )

    def summed(a, b):
        return (a.astype(jnp.float32) + b.astype(jnp.float32)).astype(jnp.bfloat16)

    got_low, got_high = moved(far_low, -1), moved(far_high, 1)
    for step in range(half - 1, 0, -1):
        mine_low, mine_high = sums[step]
        if step == half - 1:
            send_low = jnp.concatenate([summed(got_low, mine_low[:cut]), mine_low[cut:]])
            send_high = jnp.concatenate([mine_high[:cut], summed(got_high, mine_high[cut:])])
        else:
            send_low = summed(got_low, mine_low)
            send_high = summed(got_high, mine_high)
        got_low, got_high = moved(send_low, -1), moved(send_high, 1)
    (home,) = sums[0]
    mixture = (
        home.astype(jnp.float32) + got_low.astype(jnp.float32) + got_high.astype(jnp.float32)
    )
    return attended, (residual.astype(jnp.float32) + mixture).astype(jnp.bfloat16)


def slot_layer(
    queries, keys, values, kv_lengths, stream, out_weight, routes, gate_weights, own
):
    expert_gate, expert_up, expert_down = own
    row_count = queries.shape[0]
    cycle_size = lax.axis_size("ctx")
    weight_all = lax.all_gather(out_weight, "ctx", axis=0, tiled=True)
    lengths = kv_lengths
    held = 1
    while held < STOPS:
        lengths = jnp.concatenate([lengths, from_behind(lengths, "ctx", held)])
        held *= 2
    (attended,) = attend(queries, [key_window(keys, values)], lengths)
    widened, normed = project(attended, weight_all, stream)
    width = normed.shape[1]
    route_count = routes.shape[1]
    local_count = expert_gate.shape[0]
    expert_total = local_count * cycle_size
    capacity = slot_capacity(row_count, route_count, expert_total)
    flat_routes = routes.reshape(-1)
    one_hot = (flat_routes[:, None] == jnp.arange(expert_total, dtype=jnp.int32)[None, :]).astype(
        jnp.int32
    )
    earlier = jnp.cumsum(one_hot, axis=0) - one_hot
    slot_index = jnp.sum(earlier * one_hot, axis=1)
    slot_target = flat_routes * capacity + slot_index
    source_row = jnp.arange(row_count * route_count, dtype=jnp.int32) // route_count
    buffer_rows = jnp.zeros((expert_total * capacity,), jnp.int32).at[slot_target].set(source_row)
    buffer_live = jnp.zeros((expert_total * capacity,), jnp.bool_).at[slot_target].set(True)
    send_buffer = jnp.where(
        buffer_live[:, None], normed[buffer_rows], jnp.zeros((), jnp.bfloat16)
    ).reshape(expert_total, capacity, width)
    arrived = lax.all_to_all(send_buffer, "ctx", split_axis=0, concat_axis=0, tiled=True)
    by_source = arrived.reshape(cycle_size, local_count, capacity, width)
    gate_part = jnp.einsum(
        "nesd,edf->nesf", by_source, expert_gate, preferred_element_type=jnp.float32
    )
    up_part = jnp.einsum("nesd,edf->nesf", by_source, expert_up, preferred_element_type=jnp.float32)
    hidden = (jax.nn.silu(gate_part) * up_part).astype(jnp.bfloat16)
    produced = jnp.einsum(
        "nesf,efd->nesd", hidden, expert_down, preferred_element_type=jnp.float32
    ).astype(jnp.bfloat16)
    returned = lax.all_to_all(
        produced.reshape(cycle_size * local_count, capacity, width),
        "ctx",
        split_axis=0,
        concat_axis=0,
        tiled=True,
    )
    gathered = returned.reshape(expert_total * capacity, width)[slot_target].reshape(
        row_count, route_count, width
    )
    mixture = jnp.zeros((row_count, width), jnp.float32)
    for route in range(route_count):
        mixture = mixture + gate_weights[:, route : route + 1] * gathered[:, route].astype(
            jnp.float32
        )
    return attended, (widened + mixture).astype(jnp.bfloat16)


def slot_capacity(row_count, route_count, expert_total):
    return max(2, row_count * route_count * 9 // (8 * expert_total))


def shards(
    queries,
    keys,
    values,
    kv_lengths,
    stream,
    out_weight,
    routes,
    gate_weights,
    expert_gate,
    expert_up,
    expert_down,
):
    rows = queries.shape[0]
    devices = lax.axis_size("ctx")
    local_count = expert_gate.shape[0]
    capacity = slot_capacity(rows, routes.shape[1], local_count * devices)
    crowded = local_count == 1 and 4 * capacity > rows and devices % (4 * CORES) == 0
    crowded = crowded and out_weight.shape[0] == HD
    layer = ring_layer if crowded else slot_layer
    return layer(
        queries,
        keys,
        values,
        kv_lengths,
        stream,
        out_weight,
        routes,
        gate_weights,
        (expert_gate, expert_up, expert_down),
    )


def solution(mesh):
    return jax.shard_map(
        shards,
        mesh=mesh,
        in_specs=(
            P(("groups", "ctx"), None),
            P(("groups", "ctx"), None),
            P(("groups", "ctx"), None),
            P(("groups", "ctx")),
            P(("groups", "ctx"), None),
            P("ctx", None),
            P(("groups", "ctx"), None),
            P(("groups", "ctx"), None),
            P("ctx", None, None),
            P("ctx", None, None),
            P("ctx", None, None),
        ),
        out_specs=(P(("groups", "ctx"), None), P(("groups", "ctx"), None)),
        check_vma=False,
    )
```

```python
import functools
import math

import jax
import jax.numpy as jnp
from jax import lax
from jax.experimental import pallas as pl
from jax.experimental.pallas import tpu as pltpu
from jax.sharding import PartitionSpec as P


HD = 128
STOPS = 8
CORES = 2
DEAD = 1e30


def from_behind(block, axis, distance):
    devices = range(lax.axis_size(axis))
    route = [(i - distance, i) for i in devices if i - distance in devices]
    return lax.ppermute(block, axis, route)


def attend_kernel(heads, parts, length_ref, core_ref, q_ref, *refs):
    k_refs, v_refs, rest = refs[:parts], refs[parts : 2 * parts], refs[2 * parts :]
    o_ref, split_refs, bias_ref = rest[0], rest[1:-1], rest[-1]
    stops = length_ref.shape[0]
    kv_rows = bias_ref.shape[1] // stops
    rows = q_ref.shape[0]

    @pl.when(pl.program_id(0) == 0)
    def _():
        if split_refs:
            first_lane = lax.broadcasted_iota(jnp.int32, (16, HD), 1) == 0
            marks = lax.dot_general(
                first_lane.astype(jnp.float32).astype(jnp.bfloat16),
                jnp.concatenate([v_ref[...] for v_ref in v_refs], axis=0),
                (((1,), (1,)), ((), ())),
                preferred_element_type=jnp.float32,
            )[:1]
        row = lax.broadcasted_iota(jnp.int32, (1, kv_rows), 1)
        for stop in range(stops):
            part = slice(stop * kv_rows, (stop + 1) * kv_rows)
            if split_refs:
                dead = (marks[:, part] > DEAD / 2) | (row < kv_rows * (1 - length_ref[stop]))
            else:
                dead = row >= length_ref[stop]
            bias_ref[:, part] = jnp.where(dead, -1e30, 0.0)

    stacked = jnp.concatenate([q_ref[:, h * HD : (h + 1) * HD] for h in range(heads)], axis=0)
    scores = lax.dot_general(
        stacked,
        jnp.concatenate([k_ref[...] for k_ref in k_refs], axis=0),
        (((1,), (1,)), ((), ())),
        preferred_element_type=jnp.float32,
    )
    scores = scores * (HD ** (-0.5) * math.log2(math.e)) + bias_ref[...]
    highest = jnp.max(scores, axis=-1, keepdims=True)
    weights = jnp.exp2(scores - highest)
    total = jnp.sum(weights, axis=-1, keepdims=True)
    out = jnp.dot(
        weights.astype(jnp.bfloat16),
        jnp.concatenate([v_ref[...] for v_ref in v_refs], axis=0),
        preferred_element_type=jnp.float32,
    )
    out = (out / total).astype(o_ref.dtype)
    for h in range(heads):
        o_ref[:, h * HD : (h + 1) * HD] = out[h * rows : (h + 1) * rows]
    if split_refs:
        mine_ref, theirs_ref = split_refs
        first = core_ref[0] == 0
        mine_ref[...] = jnp.where(first, out[:rows], out[rows:])
        theirs_ref[...] = jnp.where(first, out[rows:], out[:rows])


def attend(queries, windows, lengths, core=None):
    rows, width = queries.shape
    kv_rows = sum(window.shape[0] for window in windows)
    kv_width = windows[0].shape[1]
    kv_heads = kv_width // (2 * HD)
    heads = width // HD
    pair = 2 if heads // kv_heads % 2 == 0 else 1
    group = heads // kv_heads // pair
    split = core is not None
    number = core if split else jnp.zeros((), jnp.int32)
    outs = [jax.ShapeDtypeStruct((rows, width), jnp.bfloat16)]
    outs += [jax.ShapeDtypeStruct((rows, width // 2), jnp.bfloat16)] * (2 * split)
    out_specs = [pl.BlockSpec((rows, pair * HD), lambda h, n, c: (0, h))]
    out_specs += [pl.BlockSpec((rows, HD), lambda h, n, c: (0, h))] * (2 * split)
    specs = [pl.BlockSpec((rows, pair * HD), lambda h, n, c: (0, h))]
    for first in (0, kv_heads):
        for window in windows:
            specs.append(
                pl.BlockSpec(
                    (window.shape[0], HD), lambda h, n, c, first=first: (0, first + h // group)
                )
            )
    return pl.pallas_call(
        functools.partial(attend_kernel, pair, len(windows)),
        grid_spec=pltpu.PrefetchScalarGridSpec(
            num_scalar_prefetch=2,
            grid=(heads // pair,),
            in_specs=specs,
            out_specs=out_specs,
            scratch_shapes=[pltpu.VMEM((1, kv_rows), jnp.float32)],
        ),
        out_shape=outs,
        compiler_params=pltpu.CompilerParams(vmem_limit_bytes=20 * 1024 * 1024),
        cost_estimate=pl.CostEstimate(
            flops=4 * rows * width * kv_rows,
            transcendentals=rows * heads * kv_rows,
            bytes_accessed=2 * (2 * rows * width + kv_rows * kv_width),
        ),
        name="attend",
    )(lengths, number.reshape(1), queries, *windows, *windows)


def key_window(keys, values):
    window = jnp.concatenate([keys, values], axis=1)
    held = 1
    while held < STOPS:
        window = jnp.concatenate([window, from_behind(window, "ctx", held)], axis=0)
        held *= 2
    return window


def expert_kernel(count, first, *refs):
    x_refs = refs[:count]
    factor_ref = refs[count]
    trios = (refs[count + 1 : count + 4], refs[count + 4 : count + 7])
    o_refs = refs[count + 7 :]
    x = jnp.concatenate([x_ref[...] for x_ref in x_refs], axis=0)
    scale = factor_ref[first : first + x.shape[0], :]
    total = None
    for column, (gate_ref, up_ref, down_ref) in enumerate(trios):
        gate = jnp.dot(x, gate_ref[0], preferred_element_type=jnp.float32)
        up = jnp.dot(x, up_ref[0], preferred_element_type=jnp.float32)
        hidden = gate / (1.0 + jnp.exp(-gate)) * up * scale[:, column : column + 1]
        part = jnp.dot(hidden.astype(jnp.bfloat16), down_ref[0], preferred_element_type=jnp.float32)
        total = part if total is None else total + part
    low = 0
    for o_ref in o_refs:
        high = low + o_ref.shape[0]
        o_ref[...] = total[low:high].astype(o_ref.dtype)
        low = high


def run_experts(blocks, factors, first, own, other):
    width = blocks[0].shape[1]
    hidden = own[0].shape[2]
    rows = sum(block.shape[0] for block in blocks)
    count = len(blocks)
    held = pl.BlockSpec(memory_space=pltpu.VMEM)
    return pl.pallas_call(
        functools.partial(expert_kernel, count, first),
        in_specs=[held] * (count + 7),
        out_specs=[held] * count,
        out_shape=[jax.ShapeDtypeStruct(block.shape, jnp.bfloat16) for block in blocks],
        compiler_params=pltpu.CompilerParams(vmem_limit_bytes=20 * 1024 * 1024),
        cost_estimate=pl.CostEstimate(
            flops=12 * rows * width * hidden,
            transcendentals=2 * rows * hidden,
            bytes_accessed=12 * width * hidden + 4 * rows * width,
        ),
        name="experts",
    )(*blocks, factors, *own, *other)


def project(attended, weight, stream):
    projected = jnp.dot(attended, weight, preferred_element_type=jnp.float32)
    residual = (stream.astype(jnp.float32) + projected).astype(jnp.bfloat16)
    widened = residual.astype(jnp.float32)
    normed = (
        widened * lax.rsqrt(jnp.mean(widened * widened, axis=-1, keepdims=True) + 1e-06)
    ).astype(jnp.bfloat16)
    return widened, normed


def project_kernel(count, sums, order_ref, *refs):
    row_refs, refs = refs[:count], refs[count:]
    sum_refs, refs = refs[:sums], refs[sums:]
    pieces, o_refs = refs[:-count], refs[-count:]
    rows = row_refs[0].shape[0]
    total = jnp.concatenate([sum_ref[...] for sum_ref in sum_refs], axis=0) if sums else None
    for index in range(0, len(pieces), 2):
        columns = []
        for place in (index, index + 1):
            low = pl.multiple_of(order_ref[place] * HD, HD)
            columns.append(
                jnp.concatenate([row_ref[:, pl.ds(low, HD)] for row_ref in row_refs], axis=0)
            )
        part = jnp.dot(
            jnp.concatenate(columns, axis=1),
            jnp.concatenate([pieces[index][...], pieces[index + 1][...]], axis=0),
            preferred_element_type=jnp.float32,
        )
        total = part if total is None else total + part
    for i, o_ref in enumerate(o_refs):
        o_ref[...] = total[i * rows : (i + 1) * rows].astype(o_ref.dtype)


def project_pieces(blocks, pieces, order, sums=()):
    rows = blocks[0].shape[0]
    width = pieces[0].shape[1]
    part = 512 if width % 512 == 0 else width
    whole = pl.BlockSpec(blocks[0].shape, lambda i, n: (0, 0))
    wide = pl.BlockSpec((rows, part), lambda i, n: (0, i))
    like = jax.ShapeDtypeStruct((rows, width), jnp.float32)
    count = len(blocks)
    return pl.pallas_call(
        functools.partial(project_kernel, count, len(sums)),
        grid_spec=pltpu.PrefetchScalarGridSpec(
            num_scalar_prefetch=1,
            grid=(width // part,),
            in_specs=[whole] * count
            + [wide] * len(sums)
            + [pl.BlockSpec((piece.shape[0], part), lambda i, n: (0, i)) for piece in pieces],
            out_specs=[wide] * count,
        ),
        out_shape=[like] * count,
        compiler_params=pltpu.CompilerParams(vmem_limit_bytes=20 * 1024 * 1024),
        cost_estimate=pl.CostEstimate(
            flops=2 * count * rows * width * len(pieces) * HD,
            transcendentals=0,
            bytes_accessed=2 * len(pieces) * HD * width + 4 * count * rows * width,
        ),
        name="project",
    )(order, *blocks, *sums, *pieces)


def whole(arrays):
    return [pl.BlockSpec(array.shape, lambda i: (0, 0)) for array in arrays]


def project_last(blocks, sums, pieces, order):
    count = len(blocks)
    outs = [sums[0], jax.ShapeDtypeStruct(sums[0].shape, jnp.bfloat16)]
    return pl.pallas_call(
        functools.partial(project_kernel, count, count),
        grid=(1,),
        in_specs=[pl.BlockSpec(memory_space=pltpu.SMEM)] + whole([*blocks, *sums, *pieces]),
        out_specs=whole(outs),
        out_shape=[jax.ShapeDtypeStruct(out.shape, out.dtype) for out in outs],
        compiler_params=pltpu.CompilerParams(vmem_limit_bytes=20 * 1024 * 1024),
        name="project_last",
    )(order, *blocks, *sums, *pieces)


def norm_kernel(stream_ref, keep_ref, got_ref, residual_ref, normed_ref):
    total = stream_ref[...].astype(jnp.float32) + keep_ref[...] + got_ref[...].astype(jnp.float32)
    residual = total.astype(jnp.bfloat16)
    residual_ref[...] = residual
    widened = residual.astype(jnp.float32)
    square = jnp.mean(widened * widened, axis=-1, keepdims=True)
    normed_ref[...] = (widened * lax.rsqrt(square + 1e-06)).astype(jnp.bfloat16)


def add_norm(stream, keep, got):
    like = jax.ShapeDtypeStruct(stream.shape, jnp.bfloat16)
    return pl.pallas_call(
        norm_kernel,
        grid=(1,),
        in_specs=whole([stream, keep, got]),
        out_specs=whole([like, like]),
        out_shape=[like, like],
        compiler_params=pltpu.CompilerParams(vmem_limit_bytes=20 * 1024 * 1024),
        name="add_norm",
    )(stream, keep, got)


def chip_ring(devices):
    chips = devices // CORES
    return list(range(0, chips, 2)) + list(range(1, chips, 2))[::-1]


def ring_layer(
    queries, keys, values, kv_lengths, stream, out_weight, routes, gate_weights, own
):
    rows = queries.shape[0]
    devices = lax.axis_size("ctx")
    here = lax.axis_index("ctx")
    ring = chip_ring(devices)
    span = len(ring)
    half = span // 2
    core, side = here % 2, here // 2 % 2
    flip = [[(i, i ^ bit) for i in range(devices)] for bit in (1, 2)]

    def moved(block, distance):
        route = [
            (ring[i] * CORES + c, ring[(i + distance) % span] * CORES + c)
            for i in range(span)
            for c in range(CORES)
        ]
        return lax.ppermute(block, "ctx", route)

    def swapped(block):
        return lax.ppermute(block, "ctx", flip[0])

    def far_memory(array):
        return pltpu.with_memory_space_constraint(array, pltpu.HBM)

    def near_memory(arrays):
        return [pltpu.with_memory_space_constraint(array, pltpu.VMEM) for array in arrays]

    chip = here // CORES
    my_place = jnp.where(chip % 2 == 0, chip // 2, span - 1 - chip // 2)
    offsets = [0] + [s * k for k in range(1, half) for s in (-1, 1)] + [half]
    places = (my_place + jnp.array(offsets, jnp.int32)) % span
    chips = jnp.where(places < half, 2 * places, 2 * (span - 1 - places) + 1)
    order = chips * CORES + core
    near = jnp.array([0, 4, 2, 6, 1, 5, 3, 7], jnp.int32)
    far = jnp.array([0, 4, 2, 6, 7, 3, 1, 5], jnp.int32)
    reached = (here - jnp.where(core == 1, near, far) >= 0).astype(jnp.int32)

    kv_rows = keys.shape[0]
    live = jnp.arange(kv_rows, dtype=jnp.int32)[:, None] < kv_lengths[0]
    expert = jnp.arange(devices, dtype=jnp.int32)
    named = routes.T[None] == expert[:, None, None]
    factor = jnp.sum(jnp.where(named, gate_weights.T[None], 0.0), axis=1)
    factor_swap = factor.reshape(devices // 2, 2, rows)[:, ::-1].reshape(devices, rows)
    notes = jnp.stack([factor, factor_swap], axis=1)

    ahead, back = moved(out_weight, 1), moved(out_weight, -1)
    mine = jnp.concatenate([keys, jnp.where(live, values, DEAD).astype(values.dtype)], axis=1)
    second = from_behind(mine, "ctx", 4)
    pieces = [out_weight]
    second, ahead, back, *late = lax.optimization_barrier((second, ahead, back, *own))
    fourth = from_behind(second, "ctx", 4)
    crossed = lax.ppermute(jnp.where(side == 0, mine, second), "ctx", flip[1])
    fourth, crossed = lax.optimization_barrier((fourth, crossed))
    crossed_far = lax.ppermute(jnp.where(side == 0, second, fourth), "ctx", flip[1])
    other = [swapped(weight) for weight in late]
    notes = lax.all_to_all(notes, "ctx", split_axis=0, concat_axis=0, tiled=True)
    for step in range(2, half + 1):
        pieces += [far_memory(ahead), far_memory(back)]
        if step == half:
            break
        ahead, back = moved(ahead, 1), moved(back, -1)
        ahead, back = lax.optimization_barrier((ahead, back))
    windows = [mine, second, crossed, crossed_far]
    shared = [jnp.where(core == 0, mine, fourth), second, crossed, crossed_far]
    windows += [swapped(window) for window in shared]
    chosen = (order[:, None] == expert[None])[:, :, None, None]
    picked = jnp.sum(jnp.where(chosen, notes[None], 0.0), axis=1)
    picked = picked.transpose(0, 2, 1).reshape(-1, 2)

    picked, reached = lax.optimization_barrier((picked, reached))
    attended, kept, given = attend(queries, windows, reached, core)
    got = swapped(given)
    ahead, attended = lax.optimization_barrier((ahead, attended))
    last = moved(ahead, 1)
    keep, give = project_pieces([kept, got], pieces[:-1], chips)
    last_two = [pieces[-1], last]
    keep, give, last_two = lax.optimization_barrier((keep, give, last_two))
    own, other = near_memory(own), near_memory(other)
    keep, give = project_last([kept, got], [keep, give], last_two, chips[-2:])
    residual, normed = add_norm(stream, keep, swapped(give))

    cut = rows // 2
    (home,) = run_experts([normed], picked, 0, own, other)
    ahead, back = normed, normed
    done = [home]
    sums = []
    for step in range(1, half):
        ahead, back = moved(ahead, 1), moved(back, -1)
        ahead, back, *done = lax.optimization_barrier((ahead, back, *done))
        sums.append(done)
        done = run_experts([ahead, back], picked, (2 * step - 1) * rows, own, other)
    far_low, far_high = moved(ahead[:cut], 1), moved(back[cut:], -1)
    far_low, far_high, *done = lax.optimization_barrier((far_low, far_high, *done))
    sums.append(done)
    far_low, far_high = run_experts(
        [far_low, far_high], picked, (2 * half - 1) * rows, own, other
    )

    def summed(a, b):
        return (a.astype(jnp.float32) + b.astype(jnp.float32)).astype(jnp.bfloat16)

    got_low, got_high = moved(far_low, -1), moved(far_high, 1)
    for step in range(half - 1, 0, -1):
        mine_low, mine_high = sums[step]
        if step == half - 1:
            send_low = jnp.concatenate([summed(got_low, mine_low[:cut]), mine_low[cut:]])
            send_high = jnp.concatenate([mine_high[:cut], summed(got_high, mine_high[cut:])])
        else:
            send_low = summed(got_low, mine_low)
            send_high = summed(got_high, mine_high)
        got_low, got_high = moved(send_low, -1), moved(send_high, 1)
    (home,) = sums[0]
    mixture = (
        home.astype(jnp.float32) + got_low.astype(jnp.float32) + got_high.astype(jnp.float32)
    )
    return attended, (residual.astype(jnp.float32) + mixture).astype(jnp.bfloat16)


def slot_layer(
    queries, keys, values, kv_lengths, stream, out_weight, routes, gate_weights, own
):
    expert_gate, expert_up, expert_down = own
    row_count = queries.shape[0]
    cycle_size = lax.axis_size("ctx")
    weight_all = lax.all_gather(out_weight, "ctx", axis=0, tiled=True)
    lengths = kv_lengths
    held = 1
    while held < STOPS:
        lengths = jnp.concatenate([lengths, from_behind(lengths, "ctx", held)])
        held *= 2
    (attended,) = attend(queries, [key_window(keys, values)], lengths)
    widened, normed = project(attended, weight_all, stream)
    width = normed.shape[1]
    route_count = routes.shape[1]
    local_count = expert_gate.shape[0]
    expert_total = local_count * cycle_size
    capacity = slot_capacity(row_count, route_count, expert_total)
    flat_routes = routes.reshape(-1)
    one_hot = (flat_routes[:, None] == jnp.arange(expert_total, dtype=jnp.int32)[None, :]).astype(
        jnp.int32
    )
    earlier = jnp.cumsum(one_hot, axis=0) - one_hot
    slot_index = jnp.sum(earlier * one_hot, axis=1)
    slot_target = flat_routes * capacity + slot_index
    source_row = jnp.arange(row_count * route_count, dtype=jnp.int32) // route_count
    buffer_rows = jnp.zeros((expert_total * capacity,), jnp.int32).at[slot_target].set(source_row)
    buffer_live = jnp.zeros((expert_total * capacity,), jnp.bool_).at[slot_target].set(True)
    send_buffer = jnp.where(
        buffer_live[:, None], normed[buffer_rows], jnp.zeros((), jnp.bfloat16)
    ).reshape(expert_total, capacity, width)
    arrived = lax.all_to_all(send_buffer, "ctx", split_axis=0, concat_axis=0, tiled=True)
    by_source = arrived.reshape(cycle_size, local_count, capacity, width)
    gate_part = jnp.einsum(
        "nesd,edf->nesf", by_source, expert_gate, preferred_element_type=jnp.float32
    )
    up_part = jnp.einsum("nesd,edf->nesf", by_source, expert_up, preferred_element_type=jnp.float32)
    hidden = (jax.nn.silu(gate_part) * up_part).astype(jnp.bfloat16)
    produced = jnp.einsum(
        "nesf,efd->nesd", hidden, expert_down, preferred_element_type=jnp.float32
    ).astype(jnp.bfloat16)
    returned = lax.all_to_all(
        produced.reshape(cycle_size * local_count, capacity, width),
        "ctx",
        split_axis=0,
        concat_axis=0,
        tiled=True,
    )
    gathered = returned.reshape(expert_total * capacity, width)[slot_target].reshape(
        row_count, route_count, width
    )
    mixture = jnp.zeros((row_count, width), jnp.float32)
    for route in range(route_count):
        mixture = mixture + gate_weights[:, route : route + 1] * gathered[:, route].astype(
            jnp.float32
        )
    return attended, (widened + mixture).astype(jnp.bfloat16)


def slot_capacity(row_count, route_count, expert_total):
    return max(2, row_count * route_count * 9 // (8 * expert_total))


def shards(
    queries,
    keys,
    values,
    kv_lengths,
    stream,
    out_weight,
    routes,
    gate_weights,
    expert_gate,
    expert_up,
    expert_down,
):
    rows = queries.shape[0]
    devices = lax.axis_size("ctx")
    local_count = expert_gate.shape[0]
    capacity = slot_capacity(rows, routes.shape[1], local_count * devices)
    crowded = local_count == 1 and 4 * capacity > rows and devices % (4 * CORES) == 0
    crowded = crowded and out_weight.shape[0] == HD
    layer = ring_layer if crowded else slot_layer
    return layer(
        queries,
        keys,
        values,
        kv_lengths,
        stream,
        out_weight,
        routes,
        gate_weights,
        (expert_gate, expert_up, expert_down),
    )


def solution(mesh):
    return jax.shard_map(
        shards,
        mesh=mesh,
        in_specs=(
            P(("groups", "ctx"), None),
            P(("groups", "ctx"), None),
            P(("groups", "ctx"), None),
            P(("groups", "ctx")),
            P(("groups", "ctx"), None),
            P("ctx", None),
            P(("groups", "ctx"), None),
            P(("groups", "ctx"), None),
            P("ctx", None, None),
            P("ctx", None, None),
            P("ctx", None, None),
        ),
        out_specs=(P(("groups", "ctx"), None), P(("groups", "ctx"), None)),
        check_vma=False,
    )
```

```python
import functools
import math

import jax
import jax.numpy as jnp
from jax import lax
from jax.experimental import pallas as pl
from jax.experimental.pallas import tpu as pltpu
from jax.sharding import PartitionSpec as P


HD = 128
STOPS = 8
CORES = 2
DEAD = 1e30


def from_behind(block, axis, distance):
    devices = range(lax.axis_size(axis))
    route = [(i - distance, i) for i in devices if i - distance in devices]
    return lax.ppermute(block, axis, route)


def attend_kernel(heads, parts, prior, length_ref, core_ref, q_ref, *refs):
    k_refs, v_refs, rest = refs[:parts], refs[parts : 2 * parts], refs[2 * parts + prior :]
    o_ref, split_refs, bias_ref = rest[0], rest[1:-1], rest[-1]
    stops = length_ref.shape[0]
    kv_rows = bias_ref.shape[1] // stops
    rows = q_ref.shape[0]

    @pl.when(pl.program_id(0) == 0)
    def _():
        if split_refs:
            first_lane = lax.broadcasted_iota(jnp.int32, (16, HD), 1) == 0
            marks = lax.dot_general(
                first_lane.astype(jnp.float32).astype(jnp.bfloat16),
                jnp.concatenate([v_ref[...] for v_ref in v_refs], axis=0),
                (((1,), (1,)), ((), ())),
                preferred_element_type=jnp.float32,
            )[:1]
        row = lax.broadcasted_iota(jnp.int32, (1, kv_rows), 1)
        for stop in range(stops):
            part = slice(stop * kv_rows, (stop + 1) * kv_rows)
            if split_refs:
                dead = (marks[:, part] > DEAD / 2) | (row < kv_rows * (1 - length_ref[stop]))
            else:
                dead = row >= length_ref[stop]
            bias_ref[:, part] = jnp.where(dead, -1e30, 0.0)

    stacked = jnp.concatenate([q_ref[:, h * HD : (h + 1) * HD] for h in range(heads)], axis=0)
    scores = lax.dot_general(
        stacked,
        jnp.concatenate([k_ref[...] for k_ref in k_refs], axis=0),
        (((1,), (1,)), ((), ())),
        preferred_element_type=jnp.float32,
    )
    scores = scores * (HD ** (-0.5) * math.log2(math.e)) + bias_ref[...]
    highest = jnp.max(scores, axis=-1, keepdims=True)
    weights = jnp.exp2(scores - highest)
    total = jnp.sum(weights, axis=-1, keepdims=True)
    out = jnp.dot(
        weights.astype(jnp.bfloat16),
        jnp.concatenate([v_ref[...] for v_ref in v_refs], axis=0),
        preferred_element_type=jnp.float32,
    )
    out = (out / total).astype(o_ref.dtype)
    for h in range(heads):
        o_ref[:, h * HD : (h + 1) * HD] = out[h * rows : (h + 1) * rows]
    if split_refs:
        mine_ref, theirs_ref = split_refs
        first = core_ref[0] == 0
        mine_ref[...] = jnp.where(first, out[:rows], out[rows:])
        theirs_ref[...] = jnp.where(first, out[rows:], out[:rows])


def attend(queries, windows, lengths, kv_head, prior=(), core=None):
    rows, width = queries.shape
    kv_rows = sum(window.shape[0] for window in windows)
    kv_heads = windows[0].shape[1] // (2 * HD)
    heads = width // HD
    pair = 2 if heads // kv_heads % 2 == 0 else 1
    group = heads // kv_heads // pair
    split = core is not None
    number = core if split else jnp.zeros((), jnp.int32)
    first = kv_head * group
    outs = [jax.ShapeDtypeStruct((rows, width), jnp.bfloat16)]
    outs += [jax.ShapeDtypeStruct((rows, width // 2), jnp.bfloat16)] * (2 * split)
    out_specs = [pl.BlockSpec((rows, pair * HD), lambda h, n, c: (0, first + h))]
    out_specs += [pl.BlockSpec((rows, HD), lambda h, n, c: (0, first + h))] * (2 * split)
    specs = [pl.BlockSpec((rows, pair * HD), lambda h, n, c: (0, first + h))]
    for column in (kv_head, kv_heads + kv_head):
        for window in windows:
            specs.append(
                pl.BlockSpec((window.shape[0], HD), lambda h, n, c, column=column: (0, column))
            )
    inputs = len(specs) + 2
    specs += [pl.BlockSpec(memory_space=pl.ANY)] * len(prior)
    return pl.pallas_call(
        functools.partial(attend_kernel, pair, len(windows), len(prior)),
        grid_spec=pltpu.PrefetchScalarGridSpec(
            num_scalar_prefetch=2,
            grid=(group,),
            in_specs=specs,
            out_specs=out_specs,
            scratch_shapes=[pltpu.VMEM((1, kv_rows), jnp.float32)],
        ),
        out_shape=outs,
        input_output_aliases={inputs + i: i for i in range(len(prior))},
        compiler_params=pltpu.CompilerParams(vmem_limit_bytes=20 * 1024 * 1024),
        cost_estimate=pl.CostEstimate(
            flops=4 * rows * width * kv_rows // kv_heads,
            transcendentals=rows * heads * kv_rows // kv_heads,
            bytes_accessed=4 * (rows * width + kv_rows * HD),
        ),
        name="attend",
    )(lengths, number.reshape(1), queries, *windows, *windows, *prior)


def key_window(keys, values):
    window = jnp.concatenate([keys, values], axis=1)
    held = 1
    while held < STOPS:
        window = jnp.concatenate([window, from_behind(window, "ctx", held)], axis=0)
        held *= 2
    return window


def expert_kernel(count, first, *refs):
    x_refs = refs[:count]
    factor_ref = refs[count]
    trios = (refs[count + 1 : count + 4], refs[count + 4 : count + 7])
    o_refs = refs[count + 7 :]
    x = jnp.concatenate([x_ref[...] for x_ref in x_refs], axis=0)
    scale = factor_ref[first : first + x.shape[0], :]
    total = None
    for column, (gate_ref, up_ref, down_ref) in enumerate(trios):
        gate = jnp.dot(x, gate_ref[0], preferred_element_type=jnp.float32)
        up = jnp.dot(x, up_ref[0], preferred_element_type=jnp.float32)
        hidden = gate / (1.0 + jnp.exp(-gate)) * up * scale[:, column : column + 1]
        part = jnp.dot(hidden.astype(jnp.bfloat16), down_ref[0], preferred_element_type=jnp.float32)
        total = part if total is None else total + part
    low = 0
    for o_ref in o_refs:
        high = low + o_ref.shape[0]
        o_ref[...] = total[low:high].astype(o_ref.dtype)
        low = high


def run_experts(blocks, factors, first, own, other):
    width = blocks[0].shape[1]
    hidden = own[0].shape[2]
    rows = sum(block.shape[0] for block in blocks)
    count = len(blocks)
    held = pl.BlockSpec(memory_space=pltpu.VMEM)
    return pl.pallas_call(
        functools.partial(expert_kernel, count, first),
        in_specs=[held] * (count + 7),
        out_specs=[held] * count,
        out_shape=[jax.ShapeDtypeStruct(block.shape, jnp.bfloat16) for block in blocks],
        compiler_params=pltpu.CompilerParams(vmem_limit_bytes=20 * 1024 * 1024),
        cost_estimate=pl.CostEstimate(
            flops=12 * rows * width * hidden,
            transcendentals=2 * rows * hidden,
            bytes_accessed=12 * width * hidden + 4 * rows * width,
        ),
        name="experts",
    )(*blocks, factors, *own, *other)


def project(attended, weight, stream):
    projected = jnp.dot(attended, weight, preferred_element_type=jnp.float32)
    residual = (stream.astype(jnp.float32) + projected).astype(jnp.bfloat16)
    widened = residual.astype(jnp.float32)
    normed = (
        widened * lax.rsqrt(jnp.mean(widened * widened, axis=-1, keepdims=True) + 1e-06)
    ).astype(jnp.bfloat16)
    return widened, normed


def project_kernel(count, sums, order_ref, *refs):
    row_refs, refs = refs[:count], refs[count:]
    sum_refs, refs = refs[:sums], refs[sums:]
    pieces, o_refs = refs[:-count], refs[-count:]
    rows = row_refs[0].shape[0]
    total = jnp.concatenate([sum_ref[...] for sum_ref in sum_refs], axis=0) if sums else None
    for index in range(0, len(pieces), 2):
        columns = []
        for place in (index, index + 1):
            low = pl.multiple_of(order_ref[place] * HD, HD)
            columns.append(
                jnp.concatenate([row_ref[:, pl.ds(low, HD)] for row_ref in row_refs], axis=0)
            )
        part = jnp.dot(
            jnp.concatenate(columns, axis=1),
            jnp.concatenate([pieces[index][...], pieces[index + 1][...]], axis=0),
            preferred_element_type=jnp.float32,
        )
        total = part if total is None else total + part
    for i, o_ref in enumerate(o_refs):
        o_ref[...] = total[i * rows : (i + 1) * rows].astype(o_ref.dtype)


def whole(arrays):
    return [pl.BlockSpec(array.shape, lambda i: (0, 0)) for array in arrays]


def project_pieces(blocks, pieces, order):
    rows = blocks[0].shape[0]
    width = pieces[0].shape[1]
    held = pl.BlockSpec(memory_space=pltpu.VMEM)
    count = len(blocks)
    return pl.pallas_call(
        functools.partial(project_kernel, count, 0),
        in_specs=[pl.BlockSpec(memory_space=pltpu.SMEM)] + [held] * (count + len(pieces)),
        out_specs=[held] * count,
        out_shape=[
            jax.ShapeDtypeStruct((rows, width), jnp.float32),
            jax.ShapeDtypeStruct((rows, width), jnp.bfloat16),
        ],
        compiler_params=pltpu.CompilerParams(vmem_limit_bytes=20 * 1024 * 1024),
        cost_estimate=pl.CostEstimate(
            flops=2 * count * rows * width * len(pieces) * HD,
            transcendentals=0,
            bytes_accessed=2 * len(pieces) * HD * width + 4 * count * rows * width,
        ),
        name="project",
    )(order, *blocks, *pieces)


def norm_kernel(stream_ref, keep_ref, got_ref, residual_ref, normed_ref):
    total = stream_ref[...].astype(jnp.float32) + keep_ref[...] + got_ref[...].astype(jnp.float32)
    residual = total.astype(jnp.bfloat16)
    residual_ref[...] = residual
    widened = residual.astype(jnp.float32)
    square = jnp.mean(widened * widened, axis=-1, keepdims=True)
    normed_ref[...] = (widened * lax.rsqrt(square + 1e-06)).astype(jnp.bfloat16)


def add_norm(stream, keep, got):
    like = jax.ShapeDtypeStruct(stream.shape, jnp.bfloat16)
    return pl.pallas_call(
        norm_kernel,
        grid=(1,),
        in_specs=whole([stream, keep, got]),
        out_specs=whole([like, like]),
        out_shape=[like, like],
        compiler_params=pltpu.CompilerParams(vmem_limit_bytes=20 * 1024 * 1024),
        name="add_norm",
    )(stream, keep, got)


def chip_ring(devices):
    chips = devices // CORES
    return list(range(0, chips, 2)) + list(range(1, chips, 2))[::-1]


def ring_layer(
    queries, keys, values, kv_lengths, stream, out_weight, routes, gate_weights, own
):
    rows = queries.shape[0]
    devices = lax.axis_size("ctx")
    here = lax.axis_index("ctx")
    ring = chip_ring(devices)
    span = len(ring)
    half = span // 2
    core, side = here % 2, here // 2 % 2
    flip = [[(i, i ^ bit) for i in range(devices)] for bit in (1, 2)]

    def moved(block, distance):
        route = [
            (ring[i] * CORES + c, ring[(i + distance) % span] * CORES + c)
            for i in range(span)
            for c in range(CORES)
        ]
        return lax.ppermute(block, "ctx", route)

    def swapped(block):
        return lax.ppermute(block, "ctx", flip[0])

    def far_memory(array):
        return pltpu.with_memory_space_constraint(array, pltpu.HBM)

    def near_memory(arrays):
        return [pltpu.with_memory_space_constraint(array, pltpu.VMEM) for array in arrays]

    chip = here // CORES
    my_place = jnp.where(chip % 2 == 0, chip // 2, span - 1 - chip // 2)
    offsets = [0] + [s * k for k in range(1, half) for s in (-1, 1)] + [half]
    places = (my_place + jnp.array(offsets, jnp.int32)) % span
    chips = jnp.where(places < half, 2 * places, 2 * (span - 1 - places) + 1)
    order = chips * CORES + core
    near = jnp.array([0, 4, 2, 6, 1, 5, 3, 7], jnp.int32)
    far = jnp.array([0, 4, 2, 6, 7, 3, 1, 5], jnp.int32)
    reached = (here - jnp.where(core == 1, near, far) >= 0).astype(jnp.int32)

    kv_rows = keys.shape[0]
    live = jnp.arange(kv_rows, dtype=jnp.int32)[:, None] < kv_lengths[0]
    expert = jnp.arange(devices, dtype=jnp.int32)
    named = routes.T[None] == expert[:, None, None]
    factor = jnp.sum(jnp.where(named, gate_weights.T[None], 0.0), axis=1)
    factor_swap = factor.reshape(devices // 2, 2, rows)[:, ::-1].reshape(devices, rows)
    notes = jnp.stack([factor, factor_swap], axis=1)

    ahead, back = moved(out_weight, 1), moved(out_weight, -1)
    mine = jnp.concatenate([keys, jnp.where(live, values, DEAD).astype(values.dtype)], axis=1)
    second = from_behind(mine, "ctx", 4)
    pieces = [out_weight]
    second, ahead, back = lax.optimization_barrier((second, ahead, back))
    fourth = from_behind(second, "ctx", 4)
    crossed = lax.ppermute(jnp.where(side == 0, mine, second), "ctx", flip[1])
    fourth, crossed = lax.optimization_barrier((fourth, crossed))
    crossed_far = lax.ppermute(jnp.where(side == 0, second, fourth), "ctx", flip[1])
    other = [swapped(weight) for weight in own]
    notes = lax.all_to_all(notes, "ctx", split_axis=0, concat_axis=0, tiled=True)
    chosen = (order[:, None] == expert[None])[:, :, None, None]
    picked = jnp.sum(jnp.where(chosen, notes[None], 0.0), axis=1)
    picked = picked.transpose(0, 2, 1).reshape(-1, 2)

    for step in range(2, half + 1):
        pieces += [ahead, back]
        if step == half:
            break
        ahead, back = moved(ahead, 1), moved(back, -1)
        if step == 2:
            ahead, back, picked, reached = lax.optimization_barrier(
                (ahead, back, picked, reached)
            )
        else:
            ahead, back = lax.optimization_barrier((ahead, back))
    windows = [mine, second, crossed, crossed_far]
    shared = [jnp.where(core == 0, mine, fourth), second, crossed, crossed_far]
    shared[:3] = [swapped(window) for window in shared[:3]]
    windows += [*shared[:3], swapped(crossed_far)]
    kv_heads = keys.shape[1] // HD
    outs = ()
    for kv_head in range(kv_heads):
        if kv_head == kv_heads - 1:
            if outs:
                ahead, *outs = lax.optimization_barrier((ahead, *outs))
            last = moved(ahead, 1)
        outs = attend(far_memory(queries), windows, reached, kv_head, outs, core)
    attended, kept, given = outs
    got = swapped(given)
    pieces.append(last)
    own, other = near_memory(own), near_memory(other)
    keep, give = project_pieces([kept, got], pieces, chips)
    residual, normed = add_norm(stream, keep, swapped(give))

    cut = rows // 2
    (home,) = run_experts([normed], picked, 0, own, other)
    ahead, back = normed, normed
    done = [home]
    sums = []
    for step in range(1, half):
        ahead, back = moved(ahead, 1), moved(back, -1)
        ahead, *done = lax.optimization_barrier((ahead, *done))
        sums.append(done)
        done = run_experts([ahead, back], picked, (2 * step - 1) * rows, own, other)
    far_low, far_high = moved(ahead[:cut], 1), moved(back[cut:], -1)
    far_low, *done = lax.optimization_barrier((far_low, *done))
    sums.append(done)
    far_low, far_high = run_experts(
        [far_low, far_high], picked, (2 * half - 1) * rows, own, other
    )

    def summed(a, b):
        return (a.astype(jnp.float32) + b.astype(jnp.float32)).astype(jnp.bfloat16)

    got_low, got_high = moved(far_low, -1), moved(far_high, 1)
    for step in range(half - 1, 0, -1):
        mine_low, mine_high = sums[step]
        if step == half - 1:
            send_low = jnp.concatenate([summed(got_low, mine_low[:cut]), mine_low[cut:]])
            send_high = jnp.concatenate([mine_high[:cut], summed(got_high, mine_high[cut:])])
        else:
            send_low = summed(got_low, mine_low)
            send_high = summed(got_high, mine_high)
        got_low, got_high = moved(send_low, -1), moved(send_high, 1)
    (home,) = sums[0]
    mixture = (
        home.astype(jnp.float32) + got_low.astype(jnp.float32) + got_high.astype(jnp.float32)
    )
    return attended, (residual.astype(jnp.float32) + mixture).astype(jnp.bfloat16)


def slot_layer(
    queries, keys, values, kv_lengths, stream, out_weight, routes, gate_weights, own
):
    expert_gate, expert_up, expert_down = own
    row_count = queries.shape[0]
    cycle_size = lax.axis_size("ctx")
    weight_all = lax.all_gather(out_weight, "ctx", axis=0, tiled=True)
    lengths = kv_lengths
    held = 1
    while held < STOPS:
        lengths = jnp.concatenate([lengths, from_behind(lengths, "ctx", held)])
        held *= 2
    prior = ()
    window = key_window(keys, values)
    for kv_head in range(keys.shape[1] // HD):
        prior = attend(queries, [window], lengths, kv_head, prior)
    (attended,) = prior
    widened, normed = project(attended, weight_all, stream)
    width = normed.shape[1]
    route_count = routes.shape[1]
    local_count = expert_gate.shape[0]
    expert_total = local_count * cycle_size
    capacity = slot_capacity(row_count, route_count, expert_total)
    flat_routes = routes.reshape(-1)
    one_hot = (flat_routes[:, None] == jnp.arange(expert_total, dtype=jnp.int32)[None, :]).astype(
        jnp.int32
    )
    earlier = jnp.cumsum(one_hot, axis=0) - one_hot
    slot_index = jnp.sum(earlier * one_hot, axis=1)
    slot_target = flat_routes * capacity + slot_index
    source_row = jnp.arange(row_count * route_count, dtype=jnp.int32) // route_count
    buffer_rows = jnp.zeros((expert_total * capacity,), jnp.int32).at[slot_target].set(source_row)
    buffer_live = jnp.zeros((expert_total * capacity,), jnp.bool_).at[slot_target].set(True)
    send_buffer = jnp.where(
        buffer_live[:, None], normed[buffer_rows], jnp.zeros((), jnp.bfloat16)
    ).reshape(expert_total, capacity, width)
    arrived = lax.all_to_all(send_buffer, "ctx", split_axis=0, concat_axis=0, tiled=True)
    by_source = arrived.reshape(cycle_size, local_count, capacity, width)
    gate_part = jnp.einsum(
        "nesd,edf->nesf", by_source, expert_gate, preferred_element_type=jnp.float32
    )
    up_part = jnp.einsum("nesd,edf->nesf", by_source, expert_up, preferred_element_type=jnp.float32)
    hidden = (jax.nn.silu(gate_part) * up_part).astype(jnp.bfloat16)
    produced = jnp.einsum(
        "nesf,efd->nesd", hidden, expert_down, preferred_element_type=jnp.float32
    ).astype(jnp.bfloat16)
    returned = lax.all_to_all(
        produced.reshape(cycle_size * local_count, capacity, width),
        "ctx",
        split_axis=0,
        concat_axis=0,
        tiled=True,
    )
    gathered = returned.reshape(expert_total * capacity, width)[slot_target].reshape(
        row_count, route_count, width
    )
    mixture = jnp.zeros((row_count, width), jnp.float32)
    for route in range(route_count):
        mixture = mixture + gate_weights[:, route : route + 1] * gathered[:, route].astype(
            jnp.float32
        )
    return attended, (widened + mixture).astype(jnp.bfloat16)


def slot_capacity(row_count, route_count, expert_total):
    return max(2, row_count * route_count * 9 // (8 * expert_total))


def shards(
    queries,
    keys,
    values,
    kv_lengths,
    stream,
    out_weight,
    routes,
    gate_weights,
    expert_gate,
    expert_up,
    expert_down,
):
    rows = queries.shape[0]
    devices = lax.axis_size("ctx")
    local_count = expert_gate.shape[0]
    capacity = slot_capacity(rows, routes.shape[1], local_count * devices)
    crowded = local_count == 1 and 4 * capacity > rows and devices % (4 * CORES) == 0
    crowded = crowded and out_weight.shape[0] == HD
    layer = ring_layer if crowded else slot_layer
    return layer(
        queries,
        keys,
        values,
        kv_lengths,
        stream,
        out_weight,
        routes,
        gate_weights,
        (expert_gate, expert_up, expert_down),
    )


def solution(mesh):
    return jax.shard_map(
        shards,
        mesh=mesh,
        in_specs=(
            P(("groups", "ctx"), None),
            P(("groups", "ctx"), None),
            P(("groups", "ctx"), None),
            P(("groups", "ctx")),
            P(("groups", "ctx"), None),
            P("ctx", None),
            P(("groups", "ctx"), None),
            P(("groups", "ctx"), None),
            P("ctx", None, None),
            P("ctx", None, None),
            P("ctx", None, None),
        ),
        out_specs=(P(("groups", "ctx"), None), P(("groups", "ctx"), None)),
        check_vma=False,
    )
```
